256 devices in a mesh: dp: 8 (over x, core), space: 32 (over y, z).
Axes of the slice: x: 4, y: 4, z: 8, core: 2. Of those that a mesh axis runs over, the one named last changes fastest.
Arguments:
- features: bfloat16 [8, 262144, 128], P('dp', 'space'), may hold values from -6 to 6
- child_parent: int32 [8, 262144], P('dp', 'space'), may hold values from 0 to 65535, as said below
- child_code: int32 [8, 262144], P('dp', 'space'), may hold values from 0 to 7
- weight: bfloat16 [8, 128, 128], replicated, may hold values from -0.25 to 0.25
- out_grad: bfloat16 [8, 65536, 128], P('dp', 'space'), may hold values from -6 to 6
Outputs:
- parent_out: bfloat16 [8, 65536, 128], P('dp', 'space')
- feature_grad: bfloat16 [8, 262144, 128], P('dp', 'space')
- weight_grad: float32 [8, 128, 128], replicated
The draws below stay inside these ranges and needn't reach their ends.
Inputs may be any that keep to these rules, and one draw needn't show every extreme that they name: Within one window, child_parent is nondecreasing along the 8192 rows of one device of space. Parent p lies on device p // 2048 of space; at most 512 rows of one device have their parent on one device, and on every device some device receives exactly 512. No two fine octants of a window share both parent and child_code.
All inputs are finite; a program needn't handle non-finite values.
Results may differ from the reference program's by a relative error of at most 0.001.
Values may be sent and summed in bfloat16 or wider, within the bound.
A program may use at most 128 MiB of HBM per device.

```python
import jax
import jax.numpy as jnp
from jax import lax

CIN = 128
COUT = 128
CHILDREN = 8
F_DEV = 8192
PAR_DEV = 2048
FINE = 262144
PARENTS = 65536
WINDOWS = 8
GRAD_ROWS = 2097152
N_SPACE = 32


def build_window(key):
    count = N_SPACE
    share = F_DEV // count
    slots = 8 * PAR_DEV
    first, second, third = jax.random.split(key, 3)
    level = jax.random.randint(first, (count, count), 0, share + 1)
    peak = jax.random.randint(second, (count,), 0, count)
    columns = jnp.arange(count)
    level = jnp.where(columns[None, :] == peak[:, None], share, level)
    level = jnp.where(columns[None, :] == ((peak + 1) % count)[:, None], 0, level)
    sent = share + level - jnp.roll(level, -1, axis=1)
    offset = jnp.cumsum(sent, axis=0) - sent
    perms = jax.vmap(lambda sub: jax.random.permutation(sub, slots))(jax.random.split(third, count))
    row_pos = jnp.arange(F_DEV)
    inclusive = jnp.cumsum(sent, axis=1)
    target = jnp.sum(inclusive[:, None, :] <= row_pos[None, :, None], axis=2).astype(jnp.int32)
    start = jnp.take_along_axis(inclusive - sent, target, axis=1)
    place = jnp.take_along_axis(offset, target, axis=1) + row_pos[None, :] - start
    chosen = perms[target, place]
    block = jnp.arange(count)[:, None] * count + target
    keyed = jnp.sort((block * slots + chosen).reshape(-1))
    chosen = keyed % slots
    owner = keyed // slots % count
    parents = owner * PAR_DEV + chosen // 8
    codes = chosen % 8
    return (parents.astype(jnp.int32), codes.astype(jnp.int32))


def build_tree(key):
    base = jax.random.fold_in(key, 7)
    return jax.vmap(build_window)(jax.random.split(base, WINDOWS))


def draw_child_parent(key, part):
    return build_tree(key)[0]


def draw_child_code(key, part):
    return build_tree(key)[1]


def level_of(stream_key, dims, cuts, smallest, high):
    def one(axis_at, parts):
        steps = jax.random.uniform(jax.random.fold_in(jax.random.fold_in(stream_key, 6), axis_at), (parts,), jnp.float32, smallest / len(cuts), high / len(cuts))
        return jnp.repeat(jnp.exp(steps), dims[axis_at] // parts).reshape((-1,) + (1,) * (len(dims) - axis_at - 1))

    gain = one(*cuts[0])
    for cut in cuts[1:]:
        gain = gain * one(*cut)
    return gain


def scatter_about(rng, extent, width, limit, shards=(), dtype=jnp.bfloat16):
    loudness = level_of(rng, extent, shards, -0.22, 0.18) if shards else 1.0
    values = jax.random.normal(rng, extent, jnp.float32) * width * loudness
    return jnp.minimum(jnp.maximum(values, -limit), limit).astype(dtype)


def setup_inputs(seed: int = 0) -> dict:
    keys = jax.random.split(jax.random.key(seed), 6)
    features = scatter_about(keys[0], (WINDOWS, FINE, CIN), 1.0, 6.0, ((0, 8), (1, 32)))
    child_parent = draw_child_parent(jax.random.fold_in(keys[5], 71), 0)
    child_code = draw_child_code(jax.random.fold_in(keys[5], 71), 0)
    weight = scatter_about(keys[3], (CHILDREN, CIN, COUT), (4 * CIN) ** -0.5, 0.25)
    out_grad = scatter_about(keys[4], (WINDOWS, PARENTS, COUT), 1.0, 6.0, ((0, 8), (1, 32)))
    return {"features": features, "child_parent": child_parent, "child_code": child_code, "weight": weight, "out_grad": out_grad}


def reference(features, child_parent, child_code, weight, out_grad):
    weight_flat = weight.reshape(CHILDREN * CIN, COUT)

    def step(packed):
        feats, parents, kinds, grads = packed
        slot_index = parents * CHILDREN + kinds
        grid = jnp.zeros((PARENTS * CHILDREN, CIN), jnp.bfloat16).at[slot_index].set(feats)
        grid = grid.reshape(PARENTS, CHILDREN * CIN)
        result = jnp.dot(grid, weight_flat, preferred_element_type=jnp.float32).astype(jnp.bfloat16)
        parent_grad = jnp.dot(grads, weight_flat.T, preferred_element_type=jnp.float32).astype(jnp.bfloat16)
        parent_grad = parent_grad.reshape(PARENTS * CHILDREN, CIN)
        fine_grad = parent_grad[slot_index]
        term = lax.dot_general(grid, grads, (((0,), (0,)), ((), ())), preferred_element_type=jnp.float32)
        return (result, fine_grad, term)
    parent_out, feature_grad, terms = lax.map(step, (features, child_parent, child_code, out_grad))
    total = lax.optimization_barrier(jnp.sum(terms, axis=0)) / jnp.sqrt(jnp.float32(GRAD_ROWS))
    weight_grad = total.reshape(CHILDREN, CIN, COUT)
    return (parent_out, feature_grad, weight_grad)
```

```python
import jax
import jax.numpy as jnp
from jax import lax
from jax.experimental import pallas as pl
from jax.experimental.pallas import tpu as pltpu
from jax.sharding import PartitionSpec as P

MESH = pl.DeviceIdType.MESH
NY = 4
NZ = 8
NS = NY * NZ
ND = 8
CAP = 528
KINDS = 8
PAR = 2048
SLOTS = KINDS * PAR
F32 = jnp.float32
BF16 = jnp.bfloat16
I32 = jnp.int32
ANY = pl.BlockSpec(memory_space=pl.ANY)
VM = pl.BlockSpec(memory_space=pltpu.VMEM)
SM = pl.BlockSpec(memory_space=pltpu.SMEM)
VLIM = 60 * 1024 * 1024


def pack_kernel(first_ref, lo_ref, hi_ref, feat_ref, slot_ref, row_ref, blk_ref, slots_ref, rows_ref):
    d = pl.program_id(0)
    first = pl.multiple_of(first_ref[d], 16)
    lo, hi = lo_ref[d], hi_ref[d]
    blk_ref[0] = feat_ref[pl.ds(first, CAP), :]
    at, lane0 = first // 128, lax.rem(first, 128)
    turn = lax.rem(128 - lane0, 128)
    lane = lax.broadcasted_iota(I32, (8, 128), 1)
    pos = lax.broadcasted_iota(I32, (8, 128), 0) * 128 + lane
    live = (pos >= lo) & (pos < hi)
    for src, dst, marker in ((slot_ref, slots_ref, SLOTS), (row_ref, rows_ref, 0)):
        here = pltpu.roll(src[pl.ds(at, 8), :], turn, 1)
        after = pltpu.roll(src[pl.ds(at + 1, 8), :], turn, 1)
        moved = jnp.where(lane < 128 - lane0, here, after)
        moved = jnp.where(live, moved, marker)
        moved = jnp.where(pos == 1022, lo, jnp.where(pos == 1023, hi, moved))
        dst[0] = moved


def pack(first, lo, hi, feats, slot2d, row2d):
    rows = feats.shape[0]
    return pl.pallas_call(
        pack_kernel,
        out_shape=(
            jax.ShapeDtypeStruct((NS, CAP, 128), BF16),
            jax.ShapeDtypeStruct((NS, 8, 128), I32),
            jax.ShapeDtypeStruct((NS, 8, 128), I32),
        ),
        grid=(NS,),
        in_specs=[
            SM,
            SM,
            SM,
            pl.BlockSpec((rows, 128), lambda d: (0, 0)),
            pl.BlockSpec(slot2d.shape, lambda d: (0, 0)),
            pl.BlockSpec(row2d.shape, lambda d: (0, 0)),
        ],
        out_specs=(
            pl.BlockSpec((1, CAP, 128), lambda d: (d, 0, 0)),
            pl.BlockSpec((1, 8, 128), lambda d: (d, 0, 0)),
            pl.BlockSpec((1, 8, 128), lambda d: (d, 0, 0)),
        ),
        name="pack",
    )(first, lo, hi, feats, slot2d, row2d)


def exchange_kernel(grad_ref, rows_ref, slots_ref, table_ref, want_ref, got_ref, ss, rs, ys, yr, gs, gr, local):
    dp, me = lax.axis_index("dp"), lax.axis_index("space")
    y, z = me // NZ, lax.rem(me, NZ)
    barrier = pltpu.get_barrier_semaphore()

    def greet(i, c):
        pl.semaphore_signal(barrier, inc=1, device_id=(dp, lax.rem(me + i, NS)), device_id_type=MESH)
        return c

    lax.fori_loop(1, NS, greet, 0)
    pl.semaphore_wait(barrier, NS - 1)

    def slots_to(i):
        t = lax.rem(me + i, NS)
        return pltpu.make_async_remote_copy(
            slots_ref.at[t], got_ref.at[me], gs.at[i], gr.at[i], device_id=(dp, t), device_id_type=MESH
        )

    def rows_to(i):
        ty = lax.rem(y + i, NY)
        return pltpu.make_async_remote_copy(
            rows_ref.at[ty], want_ref.at[y], ys.at[i], yr.at[i], device_id=(dp, ty * NZ + z), device_id_type=MESH
        )

    own = [
        pltpu.make_async_copy(grad_ref, table_ref.at[z], local.at[0]),
        pltpu.make_async_copy(rows_ref.at[y], want_ref.at[y], local.at[1]),
        pltpu.make_async_copy(slots_ref.at[me], got_ref.at[me], local.at[2]),
    ]
    half = PAR // 2

    def hop(k, side):
        block = lax.rem(z - k + NZ, NZ) if side == 0 else lax.rem(z + k, NZ)
        to = lax.rem(z + 1, NZ) if side == 0 else lax.rem(z + NZ - 1, NZ)
        part = pl.ds(0, PAR) if k < 3 else pl.ds(side * half, half)
        src = grad_ref.at[part] if k == 0 else table_ref.at[block, part]
        return pltpu.make_async_remote_copy(
            src,
            table_ref.at[block, part],
            ss.at[side, k],
            rs.at[side, k],
            device_id=(dp, y * NZ + to),
            device_id_type=MESH,
        )

    hops = [[hop(k, side) for side in range(2)] for k in range(4)]
    for side in range(2):
        hops[0][side].start()
    for i in range(1, NY):
        rows_to(i).start()

    def start_slots(i, c):
        slots_to(i).start()
        return c

    lax.fori_loop(1, NS, start_slots, 0)
    for copy in own:
        copy.start()
    for k in range(1, 4):
        for side in range(2):
            hops[k - 1][side].wait_recv()
            hops[k][side].start()
    for side in range(2):
        hops[3][side].wait_recv()
    for k in range(4):
        for side in range(2):
            hops[k][side].wait_send()
    for i in range(1, NY):
        rows_to(i).wait()

    def end_slots(i, c):
        slots_to(i).wait()
        return c

    lax.fori_loop(1, NS, end_slots, 0)
    for copy in own:
        copy.wait()


def exchange(grad, rows, slots):
    return pl.pallas_call(
        exchange_kernel,
        out_shape=(
            jax.ShapeDtypeStruct((NZ, PAR, 128), BF16),
            jax.ShapeDtypeStruct(rows.shape, I32),
            jax.ShapeDtypeStruct(slots.shape, I32),
        ),
        in_specs=[ANY] * 3,
        out_specs=(ANY,) * 3,
        scratch_shapes=[
            pltpu.SemaphoreType.DMA((2, 4)),
            pltpu.SemaphoreType.DMA((2, 4)),
            pltpu.SemaphoreType.DMA((NY,)),
            pltpu.SemaphoreType.DMA((NY,)),
            pltpu.SemaphoreType.DMA((NS,)),
            pltpu.SemaphoreType.DMA((NS,)),
            pltpu.SemaphoreType.DMA((3,)),
        ],
        compiler_params=pltpu.CompilerParams(collective_id=1, has_side_effects=True),
        name="exchange",
    )(grad, rows, slots)


def gather_kernel(want_ref, table_ref, out_ref, wide, rowbuf):
    d = pl.program_id(0)

    @pl.when(d == 0)
    def _():
        def widen(i, c):
            at = pl.ds(pl.multiple_of(i * 512, 512), 512)
            wide[at, :] = table_ref[at, :].astype(F32)
            return c

        lax.fori_loop(0, NZ * PAR // 512, widen, 0)

    base = d * 1024
    lo, hi = want_ref[base + 1022], want_ref[base + 1023]

    def group(g, c):
        for u in range(8):
            j = g * 8 + u
            rowbuf[pl.ds(j, 1), :] = wide[pl.ds(want_ref[base + j], 1), :]
        return c

    lax.fori_loop(lo // 8, (hi + 7) // 8, group, 0)
    out_ref[0] = rowbuf[...].astype(BF16)


def gather(want, table):
    return pl.pallas_call(
        gather_kernel,
        out_shape=jax.ShapeDtypeStruct((NS, CAP, 128), BF16),
        grid=(NS,),
        in_specs=[SM, pl.BlockSpec((NZ * PAR, 128), lambda d: (0, 0))],
        out_specs=pl.BlockSpec((1, CAP, 128), lambda d: (d, 0, 0)),
        scratch_shapes=[pltpu.VMEM((NZ * PAR, 128), F32), pltpu.VMEM((CAP, 128), F32)],
        compiler_params=pltpu.CompilerParams(vmem_limit_bytes=VLIM),
        name="gather",
    )(want, table)


def owner_kernel(slot_ref, blk_ref, weight_ref, grad_ref, out_ref, term_ref, grid_ref, rowbuf):
    d = pl.program_id(0)

    @pl.when(d == 0)
    def _():
        def clear(i, c):
            grid_ref[pl.ds(pl.multiple_of(i * 512, 512), 512), :] = jnp.zeros((512, 128), F32)
            return c

        lax.fori_loop(0, SLOTS // 512, clear, 0)

    rowbuf[...] = blk_ref[0].astype(F32)
    base = d * 1024
    lo, hi = slot_ref[base + 1022], slot_ref[base + 1023]

    def group(g, c):
        for u in range(8):
            j = g * 8 + u
            grid_ref[pl.ds(slot_ref[base + j], 1), :] = rowbuf[pl.ds(j, 1), :]
        return c

    lax.fori_loop(lo // 8, (hi + 7) // 8, group, 0)

    @pl.when(d == NS - 1)
    def _():
        term_ref[...] = jnp.zeros(term_ref.shape, F32)

        def chunk(i, c):
            at = pl.ds(pl.multiple_of(i * 512, 512), 512)
            cot = grad_ref[at, :]
            total = jnp.zeros((512, 128), F32)
            for k in range(KINDS):
                kids = grid_ref[pl.ds(pl.multiple_of(k * PAR + i * 512, 512), 512), :].astype(BF16)
                total = total + jnp.dot(kids, weight_ref[k], preferred_element_type=F32)
                term_ref[k * 128 : (k + 1) * 128, :] += lax.dot_general(
                    kids, cot, (((0,), (0,)), ((), ())), preferred_element_type=F32
                )
            out_ref[at, :] = total.astype(BF16)
            return c

        lax.fori_loop(0, PAR // 512, chunk, 0)


def owner(slots, blocks, weight, grad):
    return pl.pallas_call(
        owner_kernel,
        out_shape=(
            jax.ShapeDtypeStruct((PAR, 128), BF16),
            jax.ShapeDtypeStruct((KINDS * 128, 128), F32),
        ),
        grid=(NS,),
        in_specs=[
            SM,
            pl.BlockSpec((1, CAP, 128), lambda d: (d, 0, 0)),
            pl.BlockSpec((KINDS, 128, 128), lambda d: (0, 0, 0)),
            pl.BlockSpec((PAR, 128), lambda d: (0, 0)),
        ],
        out_specs=(
            pl.BlockSpec((PAR, 128), lambda d: (0, 0)),
            pl.BlockSpec((KINDS * 128, 128), lambda d: (0, 0)),
        ),
        scratch_shapes=[pltpu.VMEM((SLOTS + 8, 128), F32), pltpu.VMEM((CAP, 128), F32)],
        compiler_params=pltpu.CompilerParams(vmem_limit_bytes=VLIM),
        name="owner",
    )(slots, blocks, weight, grad)


def total_kernel(scale, term_ref, out_ref, b1, s1, b2, s2, b3, s3, b4, s4, send, recv):
    dp, me = lax.axis_index("dp"), lax.axis_index("space")
    y, z = me // NZ, lax.rem(me, NZ)
    at_dp = lambda i: (lax.rem(dp + i, ND), me)
    at_z = lambda i: (dp, y * NZ + lax.rem(z + i, NZ))
    at_y = lambda i: (dp, lax.rem(y + i, NY) * NZ + z)
    barrier = pltpu.get_barrier_semaphore()
    for who, n in ((at_dp, ND), (at_z, NZ), (at_y, NY)):
        for i in range(1, n):
            pl.semaphore_signal(barrier, inc=1, device_id=who(i), device_id_type=MESH)
    pl.semaphore_wait(barrier, ND + NZ + NY - 3)

    def swap(phase, n, who, src, dst):
        copies = [
            pltpu.make_async_remote_copy(
                src(i), dst, send.at[phase, i], recv.at[phase, i], device_id=who(i), device_id_type=MESH
            )
            for i in range(1, n)
        ]
        for c in copies:
            c.start()
        return copies

    def end(copies):
        for c in copies:
            c.wait()

    def rows(i, n):
        return pl.ds(pl.multiple_of(i * n, n), n)

    c = swap(0, ND, at_dp, lambda i: term_ref.at[rows(lax.rem(dp + i, ND), 128)], b1.at[dp])
    b1[dp] = term_ref[rows(dp, 128), :]
    end(c)
    s1[...] = ((b1[0] + b1[1]) + (b1[2] + b1[3])) + ((b1[4] + b1[5]) + (b1[6] + b1[7]))
    c = swap(1, NZ, at_z, lambda i: s1.at[rows(lax.rem(z + i, NZ), 16)], b2.at[z])
    b2[z] = s1[rows(z, 16), :]
    end(c)
    s2[...] = ((b2[0] + b2[1]) + (b2[2] + b2[3])) + ((b2[4] + b2[5]) + (b2[6] + b2[7]))
    c = swap(2, NY, at_y, lambda i: s2, b3.at[y])
    b3[y] = s2[...]
    end(c)
    s3[...] = ((b3[0] + b3[1]) + (b3[2] + b3[3])) * scale
    c = swap(3, NZ, at_z, lambda i: s3, b4.at[rows(z, 16)])
    b4[rows(z, 16), :] = s3[...]
    end(c)
    c = swap(4, ND, at_dp, lambda i: b4, s4.at[rows(dp, 128)])
    s4[rows(dp, 128), :] = b4[...]
    end(c)
    out_ref[...] = s4[...]


def total(term, scale):
    n = KINDS * 128
    return pl.pallas_call(
        lambda *refs: total_kernel(scale, *refs),
        out_shape=jax.ShapeDtypeStruct((n, 128), F32),
        in_specs=[VM],
        out_specs=VM,
        scratch_shapes=[
            pltpu.VMEM((ND, 128, 128), F32),
            pltpu.VMEM((128, 128), F32),
            pltpu.VMEM((NZ, 16, 128), F32),
            pltpu.VMEM((16, 128), F32),
            pltpu.VMEM((NY, 16, 128), F32),
            pltpu.VMEM((16, 128), F32),
            pltpu.VMEM((128, 128), F32),
            pltpu.VMEM((n, 128), F32),
            pltpu.SemaphoreType.DMA((5, 8)),
            pltpu.SemaphoreType.DMA((5, 8)),
        ],
        compiler_params=pltpu.CompilerParams(collective_id=2, has_side_effects=True),
        name="total",
    )(term)


def fine_kernel(first_ref, lo_ref, hi_ref, back_ref, kind_ref, weight_ref, out_ref, cot):
    d = pl.program_id(0)
    first, lo, hi = first_ref[d], lo_ref[d], hi_ref[d]
    row = lax.broadcasted_iota(I32, (16, 128), 0)

    def tile(t, c):
        src = pl.ds(pl.multiple_of(t * 16, 16), 16)
        dst = pl.ds(pl.multiple_of(first + t * 16, 16), 16)
        keep = row + t * 16 < lo
        new, old = back_ref[0, src, :].astype(F32), cot[dst, :].astype(F32)
        cot[dst, :] = jnp.where(keep, old, new).astype(BF16)
        return c

    lax.fori_loop(lo // 16, (hi + 15) // 16, tile, 0)

    @pl.when(d == NS - 1)
    def _():
        def chunk(i, c):
            at = pl.ds(pl.multiple_of(i * 512, 512), 512)
            rows, kinds = cot[at, :], kind_ref[at, :]
            none = jnp.zeros((512, 128), BF16)
            placed = [jnp.where(kinds == k, rows, none) for k in range(KINDS)]
            wide = jnp.concatenate(placed, axis=1)
            out_ref[at, :] = jnp.dot(wide, weight_ref[...], preferred_element_type=F32).astype(BF16)
            return c

        lax.fori_loop(0, cot.shape[0] // 512, chunk, 0)


def fine(first, lo, hi, back, kinds, weight):
    rows = kinds.shape[0]
    return pl.pallas_call(
        fine_kernel,
        out_shape=jax.ShapeDtypeStruct((rows, 128), BF16),
        grid=(NS,),
        in_specs=[
            SM,
            SM,
            SM,
            pl.BlockSpec((1, CAP, 128), lambda d: (d, 0, 0)),
            pl.BlockSpec((rows, 128), lambda d: (0, 0)),
            pl.BlockSpec(weight.shape, lambda d: (0, 0)),
        ],
        out_specs=pl.BlockSpec((rows, 128), lambda d: (0, 0)),
        scratch_shapes=[pltpu.VMEM((rows, 128), BF16)],
        compiler_params=pltpu.CompilerParams(vmem_limit_bytes=VLIM),
        name="fine",
    )(first, lo, hi, back, kinds, weight)


def per_device(features, child_parent, child_code, weight, out_grad):
    feats, parents, codes, cotangent = features[0], child_parent[0], child_code[0], out_grad[0]
    fine_rows = feats.shape[0]
    owners = parents // PAR
    ends = jnp.sum((owners[:, None] <= jnp.arange(NS)[None, :]).astype(I32), axis=0)
    starts = jnp.concatenate([jnp.zeros((1,), I32), ends[:-1]])
    first = jnp.minimum(starts // 16 * 16, fine_rows - CAP)
    lo, hi = starts - first, ends - first
    slot = codes * PAR + lax.rem(parents, PAR)
    table_row = lax.rem(parents, NZ * PAR)
    as2d = lambda v: jnp.pad(v.reshape(fine_rows // 128, 128), ((0, 16), (0, 0)))
    blocks, slots, rows = pack(first, lo, hi, feats, as2d(slot), as2d(table_row))
    arrived = lax.all_to_all(blocks, "space", split_axis=0, concat_axis=0, tiled=True)
    table, want, got = exchange(cotangent, rows.reshape(NY, NZ * 8, 128), slots)
    reply = gather(want.reshape(-1), table.reshape(NZ * PAR, 128))
    columns = [[y * NZ + z for y in range(NY)] for z in range(NZ)]
    back = lax.all_to_all(
        reply.reshape(NY, NZ * CAP, 128), "space", split_axis=0, concat_axis=0, axis_index_groups=columns, tiled=True
    ).reshape(NS, CAP, 128)
    result, term = owner(got.reshape(-1), arrived, weight, cotangent)
    grad_rows = fine_rows * NS * lax.axis_size("dp")
    weight_grad = total(term, float(1.0 / grad_rows**0.5))
    kinds = jnp.broadcast_to(codes[:, None], (fine_rows, 128)).astype(BF16)
    weight_back = jnp.transpose(weight, (0, 2, 1)).reshape(KINDS * 128, 128)
    feature_grad = fine(first, lo, hi, back, kinds, weight_back)
    return result[None], feature_grad[None], weight_grad.reshape(KINDS, 128, 128)


def solution(mesh):
    placed = (P("dp", "space", None), P("dp", "space"), P("dp", "space"), P(), P("dp", "space", None))
    return jax.shard_map(
        per_device,
        mesh=mesh,
        in_specs=placed,
        out_specs=(P("dp", "space", None), P("dp", "space", None), P()),
        check_vma=False,
    )
```

```python
import jax
import jax.numpy as jnp
from jax import lax
from jax.experimental import pallas as pl
from jax.experimental.pallas import tpu as pltpu
from jax.sharding import PartitionSpec as P

MESH = pl.DeviceIdType.MESH
NY = 4
NZ = 8
NS = NY * NZ
ND = 8
CAP = 528
KINDS = 8
PAR = 2048
SLOTS = KINDS * PAR
F32 = jnp.float32
BF16 = jnp.bfloat16
I32 = jnp.int32
ANY = pl.BlockSpec(memory_space=pl.ANY)
VM = pl.BlockSpec(memory_space=pltpu.VMEM)
SM = pl.BlockSpec(memory_space=pltpu.SMEM)
VLIM = 60 * 1024 * 1024


def cost(us):
    return pl.CostEstimate(flops=0, bytes_accessed=int(us * 3.6e6), transcendentals=0)


def pack_kernel(parent_ref, code_ref, feat_ref, blk_ref, slots_ref, rows_ref, first_ref, lo_ref, hi_ref, par, kind):
    step = pl.program_id(0)
    n = feat_ref.shape[0]

    @pl.when(step == 0)
    def _():
        whole = parent_ref[...]
        par[0 : n // 128, :] = whole
        kind[0 : n // 128, :] = code_ref[...]
        begin = jnp.int32(0)
        for d in range(NS):
            below = jnp.sum((whole < (d + 1) * PAR).astype(F32), axis=0, keepdims=True)
            end = jnp.sum(below).astype(I32)
            first = jnp.minimum(begin // 16 * 16, n - CAP)
            first_ref[d] = first
            lo_ref[d] = begin - first
            hi_ref[d] = end - first
            begin = end

    lane = lax.broadcasted_iota(I32, (8, 128), 1)
    pos = lax.broadcasted_iota(I32, (8, 128), 0) * 128 + lane

    def block(b, c):
        d = step * NZ + b
        first = pl.multiple_of(first_ref[d], 16)
        lo, hi = lo_ref[d], hi_ref[d]
        blk_ref[b] = feat_ref[pl.ds(first, CAP), :]
        at, lane0 = first // 128, lax.rem(first, 128)
        turn = lax.rem(128 - lane0, 128)
        live = (pos >= lo) & (pos < hi)

        def moved(ref):
            here = pltpu.roll(ref[pl.ds(at, 8), :], turn, 1)
            after = pltpu.roll(ref[pl.ds(at + 1, 8), :], turn, 1)
            return jnp.where(lane < 128 - lane0, here, after)

        parents, kinds = moved(par), moved(kind)

        def marked(v, other):
            v = jnp.where(live, v, other)
            return jnp.where(pos == 1022, lo, jnp.where(pos == 1023, hi, v))

        slots_ref[b] = marked(kinds * PAR + (parents & (PAR - 1)), SLOTS)
        rows_ref[b] = marked(parents & (NZ * PAR - 1), 0)
        return c

    lax.fori_loop(0, NZ, block, 0)


def pack(parents, codes, feats):
    rows = feats.shape[0]
    whole = lambda a: pl.BlockSpec(a.shape, lambda i: (0, 0))
    return pl.pallas_call(
        pack_kernel,
        out_shape=(
            jax.ShapeDtypeStruct((NS, CAP, 128), BF16),
            jax.ShapeDtypeStruct((NS, 8, 128), I32),
            jax.ShapeDtypeStruct((NS, 8, 128), I32),
        )
        + (jax.ShapeDtypeStruct((NS,), I32),) * 3,
        grid=(NY,),
        in_specs=[whole(parents), whole(codes), whole(feats)],
        out_specs=(
            pl.BlockSpec((NZ, CAP, 128), lambda i: (i, 0, 0)),
            pl.BlockSpec((NZ, 8, 128), lambda i: (i, 0, 0)),
            pl.BlockSpec((NZ, 8, 128), lambda i: (i, 0, 0)),
            SM,
            SM,
            SM,
        ),
        scratch_shapes=[pltpu.VMEM((rows // 128 + 16, 128), I32), pltpu.VMEM((rows // 128 + 16, 128), I32)],
        compiler_params=pltpu.CompilerParams(vmem_limit_bytes=VLIM),
        cost_estimate=cost(8),
        name="pack",
    )(parents, codes, feats)


def exchange_kernel(grad_ref, rows_ref, slots_ref, table_ref, want_ref, got_ref, ss, rs, ys, yr, gs, gr, local):
    dp, me = lax.axis_index("dp"), lax.axis_index("space")
    y, z = me // NZ, lax.rem(me, NZ)
    barrier = pltpu.get_barrier_semaphore()

    def greet(i, c):
        pl.semaphore_signal(barrier, inc=1, device_id=(dp, lax.rem(me + i, NS)), device_id_type=MESH)
        return c

    lax.fori_loop(1, NS, greet, 0)
    own = [
        pltpu.make_async_copy(grad_ref, table_ref.at[z], local.at[0]),
        pltpu.make_async_copy(rows_ref.at[pl.ds(y * NZ, NZ)], want_ref.at[pl.ds(y * NZ, NZ)], local.at[1]),
        pltpu.make_async_copy(slots_ref.at[me], got_ref.at[me], local.at[2]),
    ]
    for copy in own:
        copy.start()
    pl.semaphore_wait(barrier, NS - 1)
    half = PAR // 2

    def hop(k, side, sub):
        block = lax.rem(z - k + NZ, NZ) if side == 0 else lax.rem(z + k, NZ)
        to = lax.rem(z + 1, NZ) if side == 0 else lax.rem(z + NZ - 1, NZ)
        part = pl.ds(sub * half, half)
        src = grad_ref.at[part] if k == 0 else table_ref.at[block, part]
        return pltpu.make_async_remote_copy(
            src,
            table_ref.at[block, part],
            ss.at[side, k, sub],
            rs.at[side, k, sub],
            device_id=(dp, y * NZ + to),
            device_id_type=MESH,
        )

    chain = [(k, i) for k in range(4) for i in range(2 if k < 3 else 1)]
    hops = {(k, side, i): hop(k, side, side ^ i) for k, i in chain for side in range(2)}

    def rows_to(i):
        ty = lax.rem(y + i, NY)
        return pltpu.make_async_remote_copy(
            rows_ref.at[pl.ds(ty * NZ, NZ)],
            want_ref.at[pl.ds(y * NZ, NZ)],
            ys.at[i],
            yr.at[i],
            device_id=(dp, ty * NZ + z),
            device_id_type=MESH,
        )

    def slots_to(i):
        t = lax.rem(me + i, NS)
        return pltpu.make_async_remote_copy(
            slots_ref.at[t], got_ref.at[me], gs.at[i], gr.at[i], device_id=(dp, t), device_id_type=MESH
        )

    for i in range(2):
        for side in range(2):
            hops[0, side, i].start()
    for i in range(1, NY):
        rows_to(i).start()

    def start_slots(i, c):
        slots_to(i).start()
        return c

    lax.fori_loop(1, NS, start_slots, 0)
    for k, i in chain:
        for side in range(2):
            hops[k, side, i].wait_recv()
            if (k + 1, side, i) in hops:
                hops[k + 1, side, i].start()
    for copy in hops.values():
        copy.wait_send()
    for i in range(1, NY):
        rows_to(i).wait()

    def end_slots(i, c):
        slots_to(i).wait()
        return c

    lax.fori_loop(1, NS, end_slots, 0)
    for copy in own:
        copy.wait()


def exchange(grad, rows, slots):
    ints = jax.ShapeDtypeStruct((NS, 8, 128), I32)
    dma = pltpu.SemaphoreType.DMA
    return pl.pallas_call(
        exchange_kernel,
        out_shape=(jax.ShapeDtypeStruct((NZ, PAR, 128), BF16), ints, ints),
        in_specs=[ANY] * 3,
        out_specs=(ANY,) * 3,
        scratch_shapes=[dma((2, 4, 2)), dma((2, 4, 2)), dma((NY,)), dma((NY,)), dma((NS,)), dma((NS,)), dma((3,))],
        compiler_params=pltpu.CompilerParams(collective_id=1, has_side_effects=True),
        cost_estimate=cost(50),
        name="exchange",
    )(grad, rows, slots)


def gather_kernel(group_ref, want_ref, table_ref, out0, out1, out2, out3, wide, rowbuf):
    step = pl.program_id(0)

    @pl.when(step == 0)
    def _():
        def widen(i, c):
            at = pl.ds(pl.multiple_of(i * 512, 512), 512)
            wide[at, :] = table_ref[at, :].astype(F32)
            return c

        lax.fori_loop(0, NZ * PAR // 512, widen, 0)

    for i, out in enumerate((out0, out1, out2, out3)):

        @pl.when(step == i)
        def _(i=i, out=out):
            def block(b, c):
                base = (group_ref[i] * NZ + b) * 1024
                lo, hi = want_ref[base + 1022], want_ref[base + 1023]

                def group(g, c):
                    for u in range(16):
                        j = g * 16 + u
                        rowbuf[pl.ds(j, 1), :] = wide[pl.ds(want_ref[base + j], 1), :]
                    return c

                lax.fori_loop(lo // 16, (hi + 15) // 16, group, 0)
                out[b] = rowbuf[...].astype(BF16)
                return c

            lax.fori_loop(0, NZ, block, 0)


def gather(group, want, table):
    return pl.pallas_call(
        gather_kernel,
        out_shape=(jax.ShapeDtypeStruct((NZ, CAP, 128), BF16),) * NY,
        grid=(NY,),
        in_specs=[SM, SM, pl.BlockSpec((NZ * PAR, 128), lambda i: (0, 0))],
        out_specs=(pl.BlockSpec((NZ, CAP, 128), lambda i: (0, 0, 0)),) * NY,
        scratch_shapes=[pltpu.VMEM((NZ * PAR, 128), F32), pltpu.VMEM((CAP, 128), F32)],
        compiler_params=pltpu.CompilerParams(vmem_limit_bytes=VLIM),
        cost_estimate=cost(16),
        name="gather",
    )(group, want, table)


def owner_kernel(slot_ref, blk_ref, weight_ref, grad_ref, out_ref, term_ref, grid_ref, rowbuf, acc):
    step = pl.program_id(0)

    @pl.when(step == 0)
    def _():
        def clear(i, c):
            grid_ref[pl.ds(pl.multiple_of(i * 512, 512), 512), :] = jnp.zeros((512, 128), F32)
            return c

        lax.fori_loop(0, SLOTS // 512, clear, 0)

    def block(b, c):
        rowbuf[...] = blk_ref[b].astype(F32)
        base = (step * NZ + b) * 1024
        lo, hi = slot_ref[base + 1022], slot_ref[base + 1023]

        def group(g, c):
            for u in range(16):
                j = g * 16 + u
                grid_ref[pl.ds(slot_ref[base + j], 1), :] = rowbuf[pl.ds(j, 1), :]
            return c

        lax.fori_loop(lo // 16, (hi + 15) // 16, group, 0)
        return c

    lax.fori_loop(0, NZ, block, 0)

    @pl.when(step == NY - 1)
    def _():
        acc[...] = jnp.zeros(acc.shape, F32)

        def chunk(i, c):
            at = pl.ds(pl.multiple_of(i * 512, 512), 512)
            turned = jnp.transpose(grad_ref[at, :])
            total = jnp.zeros((512, 128), F32)
            for k in range(0, KINDS, 2):
                pair = [
                    grid_ref[pl.ds(pl.multiple_of(m * PAR + i * 512, 512), 512), :].astype(BF16) for m in (k, k + 1)
                ]
                kids = jnp.concatenate(pair, axis=1)
                wide = slice(k * 128, (k + 2) * 128)
                total = total + jnp.dot(kids, weight_ref[wide, :], preferred_element_type=F32)
                acc[:, wide] += jnp.dot(turned, kids, preferred_element_type=F32)
            out_ref[at, :] = total.astype(BF16)
            return c

        lax.fori_loop(0, PAR // 512, chunk, 0)
        for k in range(KINDS):
            part = slice(k * 128, (k + 1) * 128)
            term_ref[part, :] = jnp.transpose(acc[:, part])


def owner(slots, blocks, weight, grad):
    return pl.pallas_call(
        owner_kernel,
        out_shape=(
            jax.ShapeDtypeStruct((PAR, 128), BF16),
            jax.ShapeDtypeStruct((KINDS * 128, 128), F32),
        ),
        grid=(NY,),
        in_specs=[
            SM,
            pl.BlockSpec((NZ, CAP, 128), lambda i: (i, 0, 0)),
            pl.BlockSpec((KINDS * 128, 128), lambda i: (0, 0)),
            pl.BlockSpec((PAR, 128), lambda i: (0, 0)),
        ],
        out_specs=(
            pl.BlockSpec((PAR, 128), lambda i: (0, 0)),
            pl.BlockSpec((KINDS * 128, 128), lambda i: (0, 0)),
        ),
        scratch_shapes=[
            pltpu.VMEM((SLOTS + 8, 128), F32),
            pltpu.VMEM((CAP, 128), F32),
            pltpu.VMEM((128, KINDS * 128), F32),
        ],
        compiler_params=pltpu.CompilerParams(vmem_limit_bytes=VLIM),
        cost_estimate=cost(22),
        name="owner",
    )(slots, blocks, weight, grad)


def total_kernel(scale, term_ref, out_ref, b1, s1, b2, s2, b3, s3, b4, s4, send, recv):
    dp, me = lax.axis_index("dp"), lax.axis_index("space")
    y, z = me // NZ, lax.rem(me, NZ)
    at_dp = lambda i: (lax.rem(dp + i, ND), me)
    at_z = lambda i: (dp, y * NZ + lax.rem(z + i, NZ))
    at_y = lambda i: (dp, lax.rem(y + i, NY) * NZ + z)
    barrier = pltpu.get_barrier_semaphore()
    for who, n in ((at_dp, ND), (at_z, NZ), (at_y, NY)):
        for i in range(1, n):
            pl.semaphore_signal(barrier, inc=1, device_id=who(i), device_id_type=MESH)
    pl.semaphore_wait(barrier, ND + NZ + NY - 3)

    def swap(phase, n, who, src, dst):
        copies = [
            pltpu.make_async_remote_copy(
                src(i), dst, send.at[phase, i], recv.at[phase, i], device_id=who(i), device_id_type=MESH
            )
            for i in range(1, n)
        ]
        for c in copies:
            c.start()
        return copies

    def end(copies):
        for c in copies:
            c.wait()

    def rows(i, n):
        return pl.ds(pl.multiple_of(i * n, n), n)

    c = swap(0, ND, at_dp, lambda i: term_ref.at[rows(lax.rem(dp + i, ND), 128)], b1.at[dp])
    b1[dp] = term_ref[rows(dp, 128), :]
    end(c)
    s1[...] = ((b1[0] + b1[1]) + (b1[2] + b1[3])) + ((b1[4] + b1[5]) + (b1[6] + b1[7]))
    c = swap(1, NZ, at_z, lambda i: s1.at[rows(lax.rem(z + i, NZ), 16)], b2.at[z])
    b2[z] = s1[rows(z, 16), :]
    end(c)
    s2[...] = ((b2[0] + b2[1]) + (b2[2] + b2[3])) + ((b2[4] + b2[5]) + (b2[6] + b2[7]))
    c = swap(2, NY, at_y, lambda i: s2, b3.at[y])
    b3[y] = s2[...]
    end(c)
    s3[...] = ((b3[0] + b3[1]) + (b3[2] + b3[3])) * scale
    c = swap(3, NZ, at_z, lambda i: s3, b4.at[rows(z, 16)])
    b4[rows(z, 16), :] = s3[...]
    end(c)
    c = swap(4, ND, at_dp, lambda i: b4, s4.at[rows(dp, 128)])
    s4[rows(dp, 128), :] = b4[...]
    end(c)
    out_ref[...] = s4[...]


def total(term, scale):
    n = KINDS * 128
    return pl.pallas_call(
        lambda *refs: total_kernel(scale, *refs),
        out_shape=jax.ShapeDtypeStruct((n, 128), F32),
        in_specs=[VM],
        out_specs=VM,
        scratch_shapes=[
            pltpu.VMEM((ND, 128, 128), F32),
            pltpu.VMEM((128, 128), F32),
            pltpu.VMEM((NZ, 16, 128), F32),
            pltpu.VMEM((16, 128), F32),
            pltpu.VMEM((NY, 16, 128), F32),
            pltpu.VMEM((16, 128), F32),
            pltpu.VMEM((128, 128), F32),
            pltpu.VMEM((n, 128), F32),
            pltpu.SemaphoreType.DMA((5, 8)),
            pltpu.SemaphoreType.DMA((5, 8)),
        ],
        compiler_params=pltpu.CompilerParams(collective_id=2, has_side_effects=True),
        cost_estimate=cost(33),
        name="total",
    )(term)


def fine_kernel(group_ref, first_ref, lo_ref, hi_ref, b0, b1, b2, b3, kind_ref, weight_ref, out_ref, cot):
    step = pl.program_id(0)
    row = lax.broadcasted_iota(I32, (16, 128), 0)

    for i, back_ref in enumerate((b0, b1, b2, b3)):

        @pl.when(step == 0)
        def _(i=i, back_ref=back_ref):
            def block(b, c):
                d = group_ref[i] * NZ + b
                first, lo, hi = first_ref[d], lo_ref[d], hi_ref[d]

                def tile(t, c):
                    src = pl.ds(pl.multiple_of(t * 16, 16), 16)
                    dst = pl.ds(pl.multiple_of(first + t * 16, 16), 16)
                    at = row + t * 16
                    new, old = back_ref[b, src, :].astype(F32), cot[dst, :].astype(F32)
                    cot[dst, :] = jnp.where((at >= lo) & (at < hi), new, old).astype(BF16)
                    return c

                begin, end = (lo + 15) // 16, hi // 16

                def plain(t, c):
                    src = pl.ds(pl.multiple_of(t * 16, 16), 16)
                    cot[pl.ds(pl.multiple_of(first + t * 16, 16), 16), :] = back_ref[b, src, :]
                    return c

                lax.fori_loop(begin, end, plain, 0)
                lax.fori_loop(lo // 16, jnp.minimum(lo // 16 + 1, (hi + 15) // 16), tile, 0)
                lax.fori_loop(jnp.maximum(end, lo // 16 + 1), (hi + 15) // 16, tile, 0)
                return c

            lax.fori_loop(0, NZ, block, 0)

    n = out_ref.shape[0]
    at = pl.ds(pl.multiple_of(step * n, n), n)
    rows, kinds = cot[at, :], kind_ref[...]
    upper = kinds >= 4
    quarter = jnp.where(upper, kinds - 4, kinds)
    none = jnp.zeros((n, 128), BF16)
    placed = jnp.concatenate([jnp.where(quarter == k, rows, none) for k in range(4)], axis=1)
    both = jnp.dot(placed, weight_ref[...], preferred_element_type=F32).astype(BF16)
    out_ref[...] = jnp.where(upper, both[:, 128:], both[:, :128])


def fine(group, first, lo, hi, back, kinds, weight):
    rows = kinds.shape[0]
    n = 512
    return pl.pallas_call(
        fine_kernel,
        out_shape=jax.ShapeDtypeStruct((rows, 128), BF16),
        grid=(rows // n,),
        in_specs=[SM] * 4
        + [pl.BlockSpec((NZ, CAP, 128), lambda i: (0, 0, 0), pipeline_mode=pl.Buffered(1))] * NY
        + [
            pl.BlockSpec((n, 128), lambda i: (i, 0)),
            pl.BlockSpec(weight.shape, lambda i: (0, 0)),
        ],
        out_specs=pl.BlockSpec((n, 128), lambda i: (i, 0)),
        scratch_shapes=[pltpu.VMEM((rows, 128), BF16)],
        compiler_params=pltpu.CompilerParams(vmem_limit_bytes=VLIM),
        cost_estimate=cost(16),
        name="fine",
    )(group, first, lo, hi, *back, kinds, weight)


def per_device(features, child_parent, child_code, weight, out_grad):
    feats, codes, cotangent = features[0], child_code[0], out_grad[0]
    fine_rows = feats.shape[0]
    as2d = lambda v: v.reshape(fine_rows // 128, 128)
    blocks, slots, rows, first, lo, hi = pack(as2d(child_parent[0]), as2d(codes), feats)
    table, want, got = exchange(cotangent, rows, slots)
    blocks, want = lax.optimization_barrier((blocks, want))
    arrived = lax.all_to_all(blocks, "space", split_axis=0, concat_axis=0, tiled=True)
    y = lax.axis_index("space") // NZ
    step = jnp.arange(NY, dtype=I32)
    reply = gather(lax.rem(y + step, NY), want.reshape(-1), table.reshape(NZ * PAR, 128))

    def along(v, i):
        if i == 0:
            return v
        return lax.ppermute(v, "space", [(d, (d + i * NZ) % NS) for d in range(NS)])

    back = [along(v, i) for i, v in enumerate(reply)]
    kinds = jnp.broadcast_to(codes[:, None], (fine_rows, 128)).astype(BF16)
    weight_back = jnp.transpose(weight.reshape(2, 4, 128, 128), (1, 3, 0, 2)).reshape(512, 256)
    feature_grad = fine(lax.rem(y - step + NY, NY), first, lo, hi, back, kinds, weight_back)
    got, feature_grad = lax.optimization_barrier((got, feature_grad))
    result, term = owner(got.reshape(-1), arrived, weight.reshape(KINDS * 128, 128), cotangent)
    grad_rows = fine_rows * NS * lax.axis_size("dp")
    weight_grad = total(term, float(1.0 / grad_rows**0.5))
    return result[None], feature_grad[None], weight_grad.reshape(KINDS, 128, 128)


def solution(mesh):
    placed = (P("dp", "space", None), P("dp", "space"), P("dp", "space"), P(), P("dp", "space", None))
    return jax.shard_map(
        per_device,
        mesh=mesh,
        in_specs=placed,
        out_specs=(P("dp", "space", None), P("dp", "space", None), P()),
        check_vma=False,
    )
```

```python
import jax
import jax.numpy as jnp
from jax import lax
from jax.experimental import pallas as pl
from jax.experimental.pallas import tpu as pltpu
from jax.sharding import PartitionSpec as P


MESH = pl.DeviceIdType.MESH
NY = 4
NZ = 8
NS = NY * NZ
ND = 8
CAP = 528
KINDS = 8
PAR = 2048
SLOTS = KINDS * PAR
F32 = jnp.float32
BF16 = jnp.bfloat16
I32 = jnp.int32
ANY = pl.BlockSpec(memory_space=pl.ANY)
VM = pl.BlockSpec(memory_space=pltpu.VMEM)
SM = pl.BlockSpec(memory_space=pltpu.SMEM)
VLIM = 60 * 1024 * 1024


def cost(us):
    return pl.CostEstimate(flops=0, bytes_accessed=int(us * 3.6e6), transcendentals=0)


def pack_kernel(parent_ref, code_ref, feat_ref, blk_ref, slots_ref, rows_ref, first_ref, lo_ref, hi_ref, par, kind):
    step = pl.program_id(0)
    n = feat_ref.shape[0]

    @pl.when(step == 0)
    def _():
        whole = parent_ref[...]
        par[0 : n // 128, :] = whole
        kind[0 : n // 128, :] = code_ref[...]
        begin = jnp.int32(0)
        for d in range(NS):
            below = jnp.sum((whole < (d + 1) * PAR).astype(F32), axis=0, keepdims=True)
            end = jnp.sum(below).astype(I32)
            first = jnp.minimum(begin // 16 * 16, n - CAP)
            first_ref[d] = first
            lo_ref[d] = begin - first
            hi_ref[d] = end - first
            begin = end

    lane = lax.broadcasted_iota(I32, (8, 128), 1)
    pos = lax.broadcasted_iota(I32, (8, 128), 0) * 128 + lane

    def block(b, c):
        d = step * NZ + b
        first = pl.multiple_of(first_ref[d], 16)
        lo, hi = lo_ref[d], hi_ref[d]
        blk_ref[b] = feat_ref[pl.ds(first, CAP), :]
        at, lane0 = first // 128, lax.rem(first, 128)
        turn = lax.rem(128 - lane0, 128)
        live = (pos >= lo) & (pos < hi)

        def moved(ref):
            here = pltpu.roll(ref[pl.ds(at, 8), :], turn, 1)
            after = pltpu.roll(ref[pl.ds(at + 1, 8), :], turn, 1)
            return jnp.where(lane < 128 - lane0, here, after)

        parents, kinds = moved(par), moved(kind)

        def marked(v, other):
            v = jnp.where(live, v, other)
            return jnp.where(pos == 1022, lo, jnp.where(pos == 1023, hi, v))

        slots_ref[b] = marked(kinds * PAR + (parents & (PAR - 1)), SLOTS)
        rows_ref[b] = marked((parents & (NZ * PAR - 1)) + kinds * (NZ * PAR), SLOTS * NZ)
        return c

    lax.fori_loop(0, NZ, block, 0)


def pack(parents, codes, feats):
    rows = feats.shape[0]
    whole = lambda a: pl.BlockSpec(a.shape, lambda i: (0, 0))
    return pl.pallas_call(
        pack_kernel,
        out_shape=(
            jax.ShapeDtypeStruct((NS, CAP, 128), BF16),
            jax.ShapeDtypeStruct((NS, 8, 128), I32),
            jax.ShapeDtypeStruct((NS, 8, 128), I32),
        )
        + (jax.ShapeDtypeStruct((NS,), I32),) * 3,
        grid=(NY,),
        in_specs=[whole(parents), whole(codes), whole(feats)],
        out_specs=(
            pl.BlockSpec((NZ, CAP, 128), lambda i: (i, 0, 0)),
            pl.BlockSpec((NZ, 8, 128), lambda i: (i, 0, 0)),
            pl.BlockSpec((NZ, 8, 128), lambda i: (i, 0, 0)),
            SM,
            SM,
            SM,
        ),
        scratch_shapes=[pltpu.VMEM((rows // 128 + 16, 128), I32), pltpu.VMEM((rows // 128 + 16, 128), I32)],
        compiler_params=pltpu.CompilerParams(vmem_limit_bytes=VLIM),
        cost_estimate=cost(8),
        name="pack",
    )(parents, codes, feats)


def exchange_kernel(grad_ref, rows_ref, slots_ref, blk_ref, table_ref, want_ref, got_ref, *rest):
    parts, (ss, rs, ys, yr, gs, gr, fs, fr, local) = rest[:NZ], rest[NZ:]
    dp, me = lax.axis_index("dp"), lax.axis_index("space")
    y, z = me // NZ, lax.rem(me, NZ)
    barrier = pltpu.get_barrier_semaphore()

    def greet(i, c):
        pl.semaphore_signal(barrier, inc=1, device_id=(dp, lax.rem(me + i, NS)), device_id_type=MESH)
        return c

    lax.fori_loop(1, NS, greet, 0)
    own = [
        pltpu.make_async_copy(grad_ref, table_ref.at[z], local.at[0]),
        pltpu.make_async_copy(rows_ref.at[pl.ds(y * NZ, NZ)], want_ref.at[pl.ds(y * NZ, NZ)], local.at[1]),
        pltpu.make_async_copy(slots_ref.at[me], got_ref.at[me], local.at[2]),
    ]
    for r, part in enumerate(parts):
        own.append(pltpu.make_async_copy(blk_ref.at[y * NZ + lax.rem(z + r, NZ)], part.at[y], local.at[3 + r]))
    for copy in own:
        copy.start()
    pl.semaphore_wait(barrier, NS - 1)
    half = PAR // 2

    def hop(k, side, sub):
        block = lax.rem(z - k + NZ, NZ) if side == 0 else lax.rem(z + k, NZ)
        to = lax.rem(z + 1, NZ) if side == 0 else lax.rem(z + NZ - 1, NZ)
        part = pl.ds(sub * half, half)
        src = grad_ref.at[part] if k == 0 else table_ref.at[block, part]
        return pltpu.make_async_remote_copy(
            src,
            table_ref.at[block, part],
            ss.at[side, k, sub],
            rs.at[side, k, sub],
            device_id=(dp, y * NZ + to),
            device_id_type=MESH,
        )

    chain = [(k, i) for k in range(4) for i in range(2 if k < 3 else 1)]
    hops = {(k, side, i): hop(k, side, side ^ i) for k, i in chain for side in range(2)}

    def rows_to(i):
        ty = lax.rem(y + i, NY)
        return pltpu.make_async_remote_copy(
            rows_ref.at[pl.ds(ty * NZ, NZ)],
            want_ref.at[pl.ds(y * NZ, NZ)],
            ys.at[i],
            yr.at[i],
            device_id=(dp, ty * NZ + z),
            device_id_type=MESH,
        )

    def block_to(i, r):
        ty = lax.rem(y + i, NY)
        return pltpu.make_async_remote_copy(
            blk_ref.at[ty * NZ + lax.rem(z + r, NZ)],
            parts[r].at[y],
            fs.at[i, r],
            fr.at[i, r],
            device_id=(dp, ty * NZ + z),
            device_id_type=MESH,
        )

    moves = [block_to(i, r) for r in range(NZ) for i in range(1, NY)]

    def slots_to(i):
        t = lax.rem(me + i, NS)
        return pltpu.make_async_remote_copy(
            slots_ref.at[t], got_ref.at[me], gs.at[i], gr.at[i], device_id=(dp, t), device_id_type=MESH
        )

    for i in range(2):
        for side in range(2):
            hops[0, side, i].start()
    for i in range(1, NY):
        rows_to(i).start()

    def start_slots(i, c):
        slots_to(i).start()
        return c

    lax.fori_loop(1, NS, start_slots, 0)
    for move in moves:
        move.start()
    for k, i in chain:
        for side in range(2):
            hops[k, side, i].wait_recv()
            if (k + 1, side, i) in hops:
                hops[k + 1, side, i].start()
    for copy in hops.values():
        copy.wait_send()
    for move in moves:
        move.wait()
    for i in range(1, NY):
        rows_to(i).wait()

    def end_slots(i, c):
        slots_to(i).wait()
        return c

    lax.fori_loop(1, NS, end_slots, 0)
    for copy in own:
        copy.wait()


def exchange(grad, rows, slots, blocks):
    ints = jax.ShapeDtypeStruct((NS, 8, 128), I32)
    part = jax.ShapeDtypeStruct((NY, CAP, 128), BF16)
    dma = pltpu.SemaphoreType.DMA
    sems = [(2, 4, 2), (2, 4, 2), (NY,), (NY,), (NS,), (NS,), (NY, NZ), (NY, NZ), (3 + NZ,)]
    out = pl.pallas_call(
        exchange_kernel,
        out_shape=(jax.ShapeDtypeStruct((NZ, PAR, 128), BF16), ints, ints) + (part,) * NZ,
        in_specs=[ANY] * 4,
        out_specs=(ANY,) * (3 + NZ),
        scratch_shapes=[dma(n) for n in sems],
        compiler_params=pltpu.CompilerParams(collective_id=1, has_side_effects=True),
        cost_estimate=cost(50),
        name="exchange",
    )(grad, rows, slots, blocks)
    return out[0], out[1], out[2], out[3:]


def proxy_kernel(place_ref, want_ref, codes_ref, table_ref, weight_ref, *rest):
    parts, outs = rest[:NZ], rest[NZ : NZ + NY]
    term_ref, wide, rowbuf, feats, acc, sems = rest[NZ + NY :]
    y, z = place_ref[0], place_ref[1]
    copies = [pltpu.make_async_copy(part, feats.at[r], sems.at[r]) for r, part in enumerate(parts)]
    for copy in copies:
        copy.start()
    acc[...] = jnp.zeros(acc.shape, F32)

    def widen(i, c):
        at = pl.ds(pl.multiple_of(i * 512, 512), 512)
        wide[at, :] = table_ref[at, :].astype(F32)
        return c

    lax.fori_loop(0, NZ * PAR // 512, widen, 0)
    for copy in copies:
        copy.wait()

    for i, out_ref in enumerate(outs):
        q = (y + i) & (NY - 1)

        def block(r, c, q=q, out_ref=out_ref):
            zz = (z + r) & (NZ - 1)
            at = q * NZ + zz
            base = at * 1024
            lo, hi = want_ref[base + 1022], want_ref[base + 1023]

            def group(g, c):
                for u in range(16):
                    j = g * 16 + u
                    rowbuf[pl.ds(j, 1), :] = wide[pl.ds(want_ref[base + j] & (NZ * PAR - 1), 1), :]
                return c

            lax.fori_loop(lo // 16, (hi + 15) // 16, group, 0)
            codes = jnp.transpose((codes_ref[at] >> 14).astype(F32))

            def piece(first, last):
                cols = range(first // 128, (last + 127) // 128)
                kinds = [jnp.broadcast_to(codes[: min(128, last - m * 128), m : m + 1], (min(128, last - m * 128), 128)) for m in cols]
                kinds = jnp.concatenate(kinds, axis=0)
                rows = rowbuf[first:last, :]
                none = jnp.zeros(rows.shape, F32)
                placed = [jnp.where(kinds == k, rows, none).astype(BF16) for k in range(KINDS)]
                placed = jnp.concatenate(placed, axis=1)
                grads = jnp.dot(placed, weight_ref[...], preferred_element_type=F32)
                out_ref[zz, first:last, :] = grads.astype(BF16)
                turned = jnp.transpose(feats[r, q, first:last, :])
                acc[...] += jnp.dot(turned, placed, preferred_element_type=F32)

            piece(0, 256)

            @pl.when(hi > 256)
            def _():
                piece(256, CAP)

            return c

        lax.fori_loop(0, NZ, block, 0)
    for k in range(KINDS):
        part = slice(k * 128, (k + 1) * 128)
        term_ref[part, :] = acc[:, part]


def proxy(place, want, table, weight, parts):
    return pl.pallas_call(
        proxy_kernel,
        out_shape=(jax.ShapeDtypeStruct((NZ, CAP, 128), BF16),) * NY
        + (jax.ShapeDtypeStruct((KINDS * 128, 128), F32),),
        in_specs=[SM, SM, VM, VM, VM] + [ANY] * NZ,
        out_specs=(VM,) * (NY + 1),
        scratch_shapes=[
            pltpu.VMEM((NZ * PAR, 128), F32),
            pltpu.VMEM((CAP, 128), F32),
            pltpu.VMEM((NZ, NY, CAP, 128), BF16),
            pltpu.VMEM((128, KINDS * 128), F32),
            pltpu.SemaphoreType.DMA((NZ,)),
        ],
        compiler_params=pltpu.CompilerParams(vmem_limit_bytes=VLIM),
        cost_estimate=cost(30),
        name="proxy",
    )(place, want.reshape(-1), want, table, weight, *parts)


def owner_kernel(place_ref, slot_ref, weight_ref, *rest):
    parts = rest[:NZ]
    out_ref, grid_ref, rowbuf, feats, sems = rest[NZ:]
    z = place_ref[1]
    copies = [pltpu.make_async_copy(part, feats.at[s], sems.at[s]) for s, part in enumerate(parts)]
    for copy in copies:
        copy.start()

    def clear(i, c):
        grid_ref[pl.ds(pl.multiple_of(i * 512, 512), 512), :] = jnp.zeros((512, 128), F32)
        return c

    lax.fori_loop(0, SLOTS // 512, clear, 0)

    for s in range(NZ):
        copies[s].wait()

        def block(q, c, s=s):
            base = (q * NZ + ((z - s) & (NZ - 1))) * 1024
            lo, hi = slot_ref[base + 1022], slot_ref[base + 1023]
            rowbuf[...] = feats[s, q].astype(F32)

            def group(g, c):
                for u in range(16):
                    j = g * 16 + u
                    grid_ref[pl.ds(slot_ref[base + j], 1), :] = rowbuf[pl.ds(j, 1), :]
                return c

            lax.fori_loop(lo // 16, (hi + 15) // 16, group, 0)
            return c

        lax.fori_loop(0, NY, block, 0)

    def chunk(i, c):
        total = jnp.zeros((512, 128), F32)
        for k in range(0, KINDS, 2):
            pair = [grid_ref[pl.ds(pl.multiple_of(m * PAR + i * 512, 512), 512), :].astype(BF16) for m in (k, k + 1)]
            kids = jnp.concatenate(pair, axis=1)
            total = total + jnp.dot(kids, weight_ref[k * 128 : (k + 2) * 128, :], preferred_element_type=F32)
        out_ref[pl.ds(pl.multiple_of(i * 512, 512), 512), :] = total.astype(BF16)
        return c

    lax.fori_loop(0, PAR // 512, chunk, 0)


def owner(place, slots, weight, parts):
    return pl.pallas_call(
        owner_kernel,
        out_shape=jax.ShapeDtypeStruct((PAR, 128), BF16),
        in_specs=[SM, SM, VM] + [ANY] * NZ,
        out_specs=VM,
        scratch_shapes=[
            pltpu.VMEM((SLOTS + 8, 128), F32),
            pltpu.VMEM((CAP, 128), F32),
            pltpu.VMEM((NZ, NY, CAP, 128), BF16),
            pltpu.SemaphoreType.DMA((NZ,)),
        ],
        compiler_params=pltpu.CompilerParams(vmem_limit_bytes=VLIM),
        cost_estimate=cost(18),
        name="owner",
    )(place, slots.reshape(-1), weight, *parts)


def total_kernel(scale, term_ref, out_ref, b1, s1, b2, s2, b3, s3, b4, s4, send, recv):
    dp, me = lax.axis_index("dp"), lax.axis_index("space")
    y, z = me // NZ, lax.rem(me, NZ)
    at_dp = lambda i: (lax.rem(dp + i, ND), me)
    at_z = lambda i: (dp, y * NZ + lax.rem(z + i, NZ))
    at_y = lambda i: (dp, lax.rem(y + i, NY) * NZ + z)
    barrier = pltpu.get_barrier_semaphore()
    for who, n in ((at_dp, ND), (at_z, NZ), (at_y, NY)):
        for i in range(1, n):
            pl.semaphore_signal(barrier, inc=1, device_id=who(i), device_id_type=MESH)
    pl.semaphore_wait(barrier, ND + NZ + NY - 3)

    def swap(phase, n, who, src, dst):
        copies = [
            pltpu.make_async_remote_copy(
                src(i), dst, send.at[phase, i], recv.at[phase, i], device_id=who(i), device_id_type=MESH
            )
            for i in range(1, n)
        ]
        for c in copies:
            c.start()
        return copies

    def end(copies):
        for c in copies:
            c.wait()

    def rows(i, n):
        return pl.ds(pl.multiple_of(i * n, n), n)

    c = swap(0, ND, at_dp, lambda i: term_ref.at[rows(lax.rem(dp + i, ND), 128)], b1.at[dp])
    b1[dp] = term_ref[rows(dp, 128), :]
    end(c)
    s1[...] = ((b1[0] + b1[1]) + (b1[2] + b1[3])) + ((b1[4] + b1[5]) + (b1[6] + b1[7]))
    c = swap(1, NZ, at_z, lambda i: s1.at[rows(lax.rem(z + i, NZ), 16)], b2.at[z])
    b2[z] = s1[rows(z, 16), :]
    end(c)
    s2[...] = ((b2[0] + b2[1]) + (b2[2] + b2[3])) + ((b2[4] + b2[5]) + (b2[6] + b2[7]))
    c = swap(2, NY, at_y, lambda i: s2, b3.at[y])
    b3[y] = s2[...]
    end(c)
    s3[...] = ((b3[0] + b3[1]) + (b3[2] + b3[3])) * scale
    c = swap(3, NZ, at_z, lambda i: s3, b4.at[rows(z, 16)])
    b4[rows(z, 16), :] = s3[...]
    end(c)
    c = swap(4, ND, at_dp, lambda i: b4, s4.at[rows(dp, 128)])
    s4[rows(dp, 128), :] = b4[...]
    end(c)
    out_ref[...] = s4[...]


def total(term, scale):
    n = KINDS * 128
    return pl.pallas_call(
        lambda *refs: total_kernel(scale, *refs),
        out_shape=jax.ShapeDtypeStruct((n, 128), F32),
        in_specs=[VM],
        out_specs=VM,
        scratch_shapes=[
            pltpu.VMEM((ND, 128, 128), F32),
            pltpu.VMEM((128, 128), F32),
            pltpu.VMEM((NZ, 16, 128), F32),
            pltpu.VMEM((16, 128), F32),
            pltpu.VMEM((NY, 16, 128), F32),
            pltpu.VMEM((16, 128), F32),
            pltpu.VMEM((128, 128), F32),
            pltpu.VMEM((n, 128), F32),
            pltpu.SemaphoreType.DMA((5, 8)),
            pltpu.SemaphoreType.DMA((5, 8)),
        ],
        compiler_params=pltpu.CompilerParams(collective_id=2, has_side_effects=True),
        cost_estimate=cost(33),
        name="total",
    )(term)


def unpack_kernel(place_ref, first_ref, lo_ref, hi_ref, b0, b1, b2, b3, out_ref):
    row = lax.broadcasted_iota(I32, (16, 128), 0)
    for i, back_ref in enumerate((b0, b1, b2, b3)):

        def block(b, c, i=i, back_ref=back_ref):
            d = ((place_ref[0] - i) & (NY - 1)) * NZ + b
            first, lo, hi = first_ref[d], lo_ref[d], hi_ref[d]

            def tile(t, c):
                src = pl.ds(pl.multiple_of(t * 16, 16), 16)
                dst = pl.ds(pl.multiple_of(first + t * 16, 16), 16)
                at = row + t * 16
                new, old = back_ref[b, src, :].astype(F32), out_ref[dst, :].astype(F32)
                out_ref[dst, :] = jnp.where((at >= lo) & (at < hi), new, old).astype(BF16)
                return c

            def plain(t, c):
                src = pl.ds(pl.multiple_of(t * 16, 16), 16)
                out_ref[pl.ds(pl.multiple_of(first + t * 16, 16), 16), :] = back_ref[b, src, :]
                return c

            begin, end = (lo + 15) // 16, hi // 16
            lax.fori_loop(begin, end, plain, 0)
            lax.fori_loop(lo // 16, jnp.minimum(lo // 16 + 1, (hi + 15) // 16), tile, 0)
            lax.fori_loop(jnp.maximum(end, lo // 16 + 1), (hi + 15) // 16, tile, 0)
            return c

        lax.fori_loop(0, NZ, block, 0)


def unpack(place, first, lo, hi, back, rows):
    return pl.pallas_call(
        unpack_kernel,
        out_shape=jax.ShapeDtypeStruct((rows, 128), BF16),
        in_specs=[SM] * 4 + [VM] * NY,
        out_specs=VM,
        compiler_params=pltpu.CompilerParams(vmem_limit_bytes=VLIM),
        cost_estimate=cost(8),
        name="unpack",
    )(place, first, lo, hi, *back)


def per_device(features, child_parent, child_code, weight, out_grad):
    feats, cotangent = features[0], out_grad[0]
    fine_rows = feats.shape[0]
    as2d = lambda v: v.reshape(fine_rows // 128, 128)
    blocks, slots, rows, first, lo, hi = pack(as2d(child_parent[0]), as2d(child_code[0]), feats)
    table, want, got, parts = exchange(cotangent, rows, slots, blocks)
    me = lax.axis_index("space")
    place = jnp.stack([me // NZ, lax.rem(me, NZ)])

    def along_z(v, s):
        if s == 0:
            return v
        return lax.ppermute(v, "space", [(d, d // NZ * NZ + (d + s) % NZ) for d in range(NS)])

    def along_y(v, i):
        if i == 0:
            return v
        return lax.ppermute(v, "space", [(d, (d + i * NZ) % NS) for d in range(NS)])

    arrived = [along_z(v, s) for s, v in enumerate(parts)]
    weight_back = jnp.transpose(weight, (0, 2, 1)).reshape(KINDS * 128, 128)
    *reply, term = proxy(place, want, table.reshape(NZ * PAR, 128), weight_back, parts)
    back = [along_y(v, i) for i, v in enumerate(reply)]
    grad_rows = fine_rows * NS * lax.axis_size("dp")
    weight_grad = total(term, float(1.0 / grad_rows**0.5))
    first, weight_grad = lax.optimization_barrier((first, weight_grad))
    feature_grad = unpack(place, first, lo, hi, back, fine_rows)
    got, feature_grad = lax.optimization_barrier((got, feature_grad))
    result = owner(place, got, weight.reshape(KINDS * 128, 128), arrived)
    return result[None], feature_grad[None], weight_grad.reshape(KINDS, 128, 128)


def solution(mesh):
    placed = (P("dp", "space", None), P("dp", "space"), P("dp", "space"), P(), P("dp", "space", None))
    return jax.shard_map(
        per_device,
        mesh=mesh,
        in_specs=placed,
        out_specs=(P("dp", "space", None), P("dp", "space", None), P()),
        check_vma=False,
    )
```

```python
import jax
import jax.numpy as jnp
from jax import lax
from jax.experimental import pallas as pl
from jax.experimental.pallas import tpu as pltpu
from jax.sharding import PartitionSpec as P


MESH = pl.DeviceIdType.MESH
NY = 4
NZ = 8
NS = NY * NZ
ND = 8
CAP = 528
KINDS = 8
PAR = 2048
SLOTS = KINDS * PAR
F32 = jnp.float32
BF16 = jnp.bfloat16
I32 = jnp.int32
ANY = pl.BlockSpec(memory_space=pl.ANY)
VM = pl.BlockSpec(memory_space=pltpu.VMEM)
SM = pl.BlockSpec(memory_space=pltpu.SMEM)
VLIM = 60 * 1024 * 1024


def cost(us):
    return pl.CostEstimate(flops=0, bytes_accessed=int(us * 3.6e6), transcendentals=0)


def pack_kernel(parent_ref, code_ref, feat_ref, blk_ref, slots_ref, rows_ref, first_ref, lo_ref, hi_ref, par, kind):
    step = pl.program_id(0)
    n = feat_ref.shape[0]

    @pl.when(step == 0)
    def _():
        whole = parent_ref[...]
        par[0 : n // 128, :] = whole
        kind[0 : n // 128, :] = code_ref[...]
        begin = jnp.int32(0)
        for d in range(NS):
            below = jnp.sum((whole < (d + 1) * PAR).astype(F32), axis=0, keepdims=True)
            end = jnp.sum(below).astype(I32)
            first = jnp.minimum(begin // 16 * 16, n - CAP)
            first_ref[d] = first
            lo_ref[d] = begin - first
            hi_ref[d] = end - first
            begin = end

    lane = lax.broadcasted_iota(I32, (8, 128), 1)
    pos = lax.broadcasted_iota(I32, (8, 128), 0) * 128 + lane

    def block(b, c):
        d = step * NZ + b
        first = pl.multiple_of(first_ref[d], 16)
        lo, hi = lo_ref[d], hi_ref[d]
        blk_ref[b] = feat_ref[pl.ds(first, CAP), :]
        at, lane0 = first // 128, lax.rem(first, 128)
        turn = lax.rem(128 - lane0, 128)
        live = (pos >= lo) & (pos < hi)

        def moved(ref):
            here = pltpu.roll(ref[pl.ds(at, 8), :], turn, 1)
            after = pltpu.roll(ref[pl.ds(at + 1, 8), :], turn, 1)
            return jnp.where(lane < 128 - lane0, here, after)

        parents, kinds = moved(par), moved(kind)

        def marked(v, other):
            v = jnp.where(live, v, other)
            return jnp.where(pos == 1022, lo, jnp.where(pos == 1023, hi, v))

        slots_ref[b] = marked(kinds * PAR + (parents & (PAR - 1)), SLOTS)
        rows_ref[b] = marked((parents & (NZ * PAR - 1)) + kinds * (NZ * PAR), SLOTS * NZ)
        return c

    lax.fori_loop(0, NZ, block, 0)


def pack(parents, codes, feats):
    rows = feats.shape[0]
    whole = lambda a: pl.BlockSpec(a.shape, lambda i: (0, 0))
    return pl.pallas_call(
        pack_kernel,
        out_shape=(
            jax.ShapeDtypeStruct((NS, CAP, 128), BF16),
            jax.ShapeDtypeStruct((NS, 8, 128), I32),
            jax.ShapeDtypeStruct((NS, 8, 128), I32),
        )
        + (jax.ShapeDtypeStruct((NS,), I32),) * 3,
        grid=(NY,),
        in_specs=[whole(parents), whole(codes), whole(feats)],
        out_specs=(
            pl.BlockSpec((NZ, CAP, 128), lambda i: (i, 0, 0)),
            pl.BlockSpec((NZ, 8, 128), lambda i: (i, 0, 0)),
            pl.BlockSpec((NZ, 8, 128), lambda i: (i, 0, 0)),
            SM,
            SM,
            SM,
        ),
        scratch_shapes=[pltpu.VMEM((rows // 128 + 16, 128), I32), pltpu.VMEM((rows // 128 + 16, 128), I32)],
        compiler_params=pltpu.CompilerParams(vmem_limit_bytes=VLIM),
        cost_estimate=cost(8),
        name="pack",
    )(parents, codes, feats)


def exchange_kernel(grad_ref, rows_ref, slots_ref, blk_ref, table_ref, want_ref, got_ref, *rest):
    parts, (mine, ss, rs, ys, yr, gs, gr, fs, fr, local, stage) = rest[:NZ], rest[NZ:]
    dp, me = lax.axis_index("dp"), lax.axis_index("space")
    y, z = me // NZ, lax.rem(me, NZ)
    barrier = pltpu.get_barrier_semaphore()

    def greet(i, c):
        pl.semaphore_signal(barrier, inc=1, device_id=(dp, lax.rem(me + i, NS)), device_id_type=MESH)
        return c

    lax.fori_loop(1, NS, greet, 0)
    own = [
        pltpu.make_async_copy(grad_ref, table_ref.at[z], local.at[0]),
        pltpu.make_async_copy(rows_ref.at[pl.ds(y * NZ, NZ)], want_ref.at[pl.ds(y * NZ, NZ)], local.at[1]),
        pltpu.make_async_copy(slots_ref.at[me], got_ref.at[me], local.at[2]),
    ]
    loads = [pltpu.make_async_copy(blk_ref.at[y * NZ + lax.rem(z + r, NZ)], mine.at[r], stage.at[r]) for r in range(NZ)]
    stores = [pltpu.make_async_copy(mine.at[r], parts[r].at[y], local.at[3 + r]) for r in range(NZ)]
    for copy in own + loads:
        copy.start()
    pl.semaphore_wait(barrier, NS - 1)
    half = PAR // 2

    def hop(k, side, sub):
        block = lax.rem(z - k + NZ, NZ) if side == 0 else lax.rem(z + k, NZ)
        to = lax.rem(z + 1, NZ) if side == 0 else lax.rem(z + NZ - 1, NZ)
        part = pl.ds(sub * half, half)
        src = grad_ref.at[part] if k == 0 else table_ref.at[block, part]
        return pltpu.make_async_remote_copy(
            src,
            table_ref.at[block, part],
            ss.at[side, k, sub],
            rs.at[side, k, sub],
            device_id=(dp, y * NZ + to),
            device_id_type=MESH,
        )

    chain = [(k, i) for k in range(4) for i in range(2 if k < 3 else 1)]
    hops = {(k, side, i): hop(k, side, side ^ i) for k, i in chain for side in range(2)}

    def rows_to(i):
        ty = lax.rem(y + i, NY)
        return pltpu.make_async_remote_copy(
            rows_ref.at[pl.ds(ty * NZ, NZ)],
            want_ref.at[pl.ds(y * NZ, NZ)],
            ys.at[i],
            yr.at[i],
            device_id=(dp, ty * NZ + z),
            device_id_type=MESH,
        )

    def block_to(i, r):
        ty = lax.rem(y + i, NY)
        return pltpu.make_async_remote_copy(
            blk_ref.at[ty * NZ + lax.rem(z + r, NZ)],
            parts[r].at[y],
            fs.at[i, r],
            fr.at[i, r],
            device_id=(dp, ty * NZ + z),
            device_id_type=MESH,
        )

    moves = [block_to(i, r) for r in range(NZ) for i in range(1, NY)]

    def slots_to(i):
        t = lax.rem(me + i, NS)
        return pltpu.make_async_remote_copy(
            slots_ref.at[t], got_ref.at[me], gs.at[i], gr.at[i], device_id=(dp, t), device_id_type=MESH
        )

    for i in range(2):
        for side in range(2):
            hops[0, side, i].start()
    for i in range(1, NY):
        rows_to(i).start()

    def start_slots(i, c):
        slots_to(i).start()
        return c

    lax.fori_loop(1, NS, start_slots, 0)
    for move in moves:
        move.start()
    for load, put in zip(loads, stores):
        load.wait()
        put.start()
    for k, i in chain:
        for side in range(2):
            hops[k, side, i].wait_recv()
            if (k + 1, side, i) in hops:
                hops[k + 1, side, i].start()
    for copy in hops.values():
        copy.wait_send()
    for move in moves:
        move.wait()
    for i in range(1, NY):
        rows_to(i).wait()

    def end_slots(i, c):
        slots_to(i).wait()
        return c

    lax.fori_loop(1, NS, end_slots, 0)
    for copy in own + stores:
        copy.wait()


def exchange(grad, rows, slots, blocks):
    ints = jax.ShapeDtypeStruct((NS, 8, 128), I32)
    part = jax.ShapeDtypeStruct((NY, CAP, 128), BF16)
    dma = pltpu.SemaphoreType.DMA
    sems = [(2, 4, 2), (2, 4, 2), (NY,), (NY,), (NS,), (NS,), (NY, NZ), (NY, NZ), (3 + NZ,), (NZ,)]
    out = pl.pallas_call(
        exchange_kernel,
        out_shape=(jax.ShapeDtypeStruct((NZ, PAR, 128), BF16), ints, ints) + (part,) * NZ,
        in_specs=[VM] + [ANY] * 3,
        out_specs=(VM,) + (ANY,) * (2 + NZ),
        scratch_shapes=[pltpu.VMEM((NZ, CAP, 128), BF16)] + [dma(n) for n in sems],
        compiler_params=pltpu.CompilerParams(collective_id=1, has_side_effects=True, vmem_limit_bytes=VLIM),
        cost_estimate=cost(50),
        name="exchange",
    )(grad, rows, slots, blocks)
    return out[0], out[1], out[2], out[3:]


def place():
    me = lax.axis_index("space")
    return me >> 3, me & (NZ - 1)


def proxy_kernel(distances, want_ref, codes_ref, table_ref, weight_ref, *rest):
    n = len(distances)
    parts, outs = rest[:NZ], rest[NZ : NZ + n]
    term_ref, wide, rowbuf, feats, acc, turned_weight, sems = rest[NZ + n :]
    y, z = place()
    copies = [
        pltpu.make_async_copy(part.at[(y + i) & (NY - 1)], feats.at[r, m], sems.at[r, m])
        for m, i in enumerate(distances)
        for r, part in enumerate(parts)
    ]
    for copy in copies:
        copy.start()
    acc[...] = jnp.zeros(acc.shape, F32)
    for k in range(KINDS):
        turned_weight[k * 128 : (k + 1) * 128, :] = jnp.transpose(weight_ref[k])

    def widen(i, c):
        at = pl.ds(pl.multiple_of(i * 512, 512), 512)
        wide[at, :] = table_ref[at, :].astype(F32)
        return c

    lax.fori_loop(0, NZ * PAR // 512, widen, 0)
    for copy in copies:
        copy.wait()

    for m, out_ref in enumerate(outs):
        q = (y + distances[m]) & (NY - 1)

        def block(r, c, m=m, q=q, out_ref=out_ref):
            zz = (z + r) & (NZ - 1)
            at = q * NZ + zz
            base = at * 1024
            lo, hi = want_ref[base + 1022], want_ref[base + 1023]

            def group(g, c):
                for u in range(16):
                    j = g * 16 + u
                    rowbuf[pl.ds(j, 1), :] = wide[pl.ds(want_ref[base + j] & (NZ * PAR - 1), 1), :]
                return c

            lax.fori_loop(lo // 16, (hi + 15) // 16, group, 0)
            codes = jnp.transpose((codes_ref[at] >> 14).astype(F32))

            def piece(first, last):
                cols = range(first // 128, (last + 127) // 128)
                kinds = [jnp.broadcast_to(codes[: min(128, last - m * 128), m : m + 1], (min(128, last - m * 128), 128)) for m in cols]
                kinds = jnp.concatenate(kinds, axis=0)
                rows = rowbuf[first:last, :]
                none = jnp.zeros(rows.shape, F32)
                placed = [jnp.where(kinds == k, rows, none).astype(BF16) for k in range(KINDS)]
                placed = jnp.concatenate(placed, axis=1)
                grads = jnp.dot(placed, turned_weight[...], preferred_element_type=F32)
                out_ref[zz, first:last, :] = grads.astype(BF16)
                turned = jnp.transpose(feats[r, m, first:last, :])
                acc[...] += jnp.dot(turned, placed, preferred_element_type=F32)

            piece(0, 256)

            @pl.when(hi > 256)
            def _():
                piece(256, CAP)

            return c

        lax.fori_loop(0, NZ, block, 0)
    for k in range(KINDS):
        part = slice(k * 128, (k + 1) * 128)
        term_ref[part, :] = acc[:, part]


def proxy(distances, want, table, weight, parts):
    n = len(distances)
    *rows, term = pl.pallas_call(
        lambda *refs: proxy_kernel(distances, *refs),
        out_shape=(jax.ShapeDtypeStruct((NZ, CAP, 128), BF16),) * n
        + (jax.ShapeDtypeStruct((KINDS * 128, 128), F32),),
        in_specs=[SM, VM, VM, VM] + [ANY] * NZ,
        out_specs=(VM,) * (n + 1),
        scratch_shapes=[
            pltpu.VMEM((NZ * PAR, 128), F32),
            pltpu.VMEM((CAP, 128), F32),
            pltpu.VMEM((NZ, n, CAP, 128), BF16),
            pltpu.VMEM((128, KINDS * 128), F32),
            pltpu.VMEM((KINDS * 128, 128), BF16),
            pltpu.SemaphoreType.DMA((NZ, n)),
        ],
        compiler_params=pltpu.CompilerParams(vmem_limit_bytes=VLIM),
        cost_estimate=cost(20),
        name="proxy",
    )(want.reshape(-1), want, table, weight, *parts)
    return dict(zip(distances, rows)), term


def owner_kernel(slot_ref, weight_ref, *rest):
    parts = rest[:NZ]
    out_ref, grid_ref, rowbuf, feats, sems = rest[NZ:]
    _, z = place()
    copies = [pltpu.make_async_copy(part, feats.at[s], sems.at[s]) for s, part in enumerate(parts)]
    for copy in copies:
        copy.start()

    def clear(i, c):
        grid_ref[pl.ds(pl.multiple_of(i * 512, 512), 512), :] = jnp.zeros((512, 128), F32)
        return c

    lax.fori_loop(0, SLOTS // 512, clear, 0)

    for s in range(NZ):
        copies[s].wait()

        def block(q, c, s=s):
            base = (q * NZ + ((z - s) & (NZ - 1))) * 1024
            lo, hi = slot_ref[base + 1022], slot_ref[base + 1023]
            rowbuf[...] = feats[s, q].astype(F32)

            def group(g, c):
                for u in range(16):
                    j = g * 16 + u
                    grid_ref[pl.ds(slot_ref[base + j], 1), :] = rowbuf[pl.ds(j, 1), :]
                return c

            lax.fori_loop(lo // 16, (hi + 15) // 16, group, 0)
            return c

        lax.fori_loop(0, NY, block, 0)

    def chunk(i, c):
        total = jnp.zeros((512, 128), F32)
        for k in range(0, KINDS, 2):
            pair = [grid_ref[pl.ds(pl.multiple_of(m * PAR + i * 512, 512), 512), :].astype(BF16) for m in (k, k + 1)]
            kids = jnp.concatenate(pair, axis=1)
            total = total + jnp.dot(kids, weight_ref[k * 128 : (k + 2) * 128, :], preferred_element_type=F32)
        out_ref[pl.ds(pl.multiple_of(i * 512, 512), 512), :] = total.astype(BF16)
        return c

    lax.fori_loop(0, PAR // 512, chunk, 0)


def owner(slots, weight, parts):
    return pl.pallas_call(
        owner_kernel,
        out_shape=jax.ShapeDtypeStruct((PAR, 128), BF16),
        in_specs=[SM, VM] + [ANY] * NZ,
        out_specs=VM,
        scratch_shapes=[
            pltpu.VMEM((SLOTS + 8, 128), F32),
            pltpu.VMEM((CAP, 128), F32),
            pltpu.VMEM((NZ, NY, CAP, 128), BF16),
            pltpu.SemaphoreType.DMA((NZ,)),
        ],
        compiler_params=pltpu.CompilerParams(vmem_limit_bytes=VLIM),
        cost_estimate=cost(18),
        name="owner",
    )(slots.reshape(-1), weight, *parts)


def total_kernel(scale, far_ref, near_ref, out_ref, term_ref, b1, s1, b2, s2, b3, s3, b4, s4, send, recv):
    dp, me = lax.axis_index("dp"), lax.axis_index("space")
    y, z = me // NZ, lax.rem(me, NZ)
    at_dp = lambda i: (lax.rem(dp + i, ND), me)
    at_z = lambda i: (dp, y * NZ + lax.rem(z + i, NZ))
    at_y = lambda i: (dp, lax.rem(y + i, NY) * NZ + z)
    term_ref[...] = far_ref[...] + near_ref[...]
    barrier = pltpu.get_barrier_semaphore()
    for who, n in ((at_dp, ND), (at_z, NZ), (at_y, NY)):
        for i in range(1, n):
            pl.semaphore_signal(barrier, inc=1, device_id=who(i), device_id_type=MESH)
    pl.semaphore_wait(barrier, ND + NZ + NY - 3)

    def swap(phase, n, who, src, dst):
        copies = [
            pltpu.make_async_remote_copy(
                src(i), dst, send.at[phase, i], recv.at[phase, i], device_id=who(i), device_id_type=MESH
            )
            for i in range(1, n)
        ]
        for c in copies:
            c.start()
        return copies

    def end(copies):
        for c in copies:
            c.wait()

    def rows(i, n):
        return pl.ds(pl.multiple_of(i * n, n), n)

    c = swap(0, ND, at_dp, lambda i: term_ref.at[rows(lax.rem(dp + i, ND), 128)], b1.at[dp])
    b1[dp] = term_ref[rows(dp, 128), :]
    end(c)
    s1[...] = ((b1[0] + b1[1]) + (b1[2] + b1[3])) + ((b1[4] + b1[5]) + (b1[6] + b1[7]))
    c = swap(1, NZ, at_z, lambda i: s1.at[rows(lax.rem(z + i, NZ), 16)], b2.at[z])
    b2[z] = s1[rows(z, 16), :]
    end(c)
    s2[...] = ((b2[0] + b2[1]) + (b2[2] + b2[3])) + ((b2[4] + b2[5]) + (b2[6] + b2[7]))
    c = swap(2, NY, at_y, lambda i: s2, b3.at[y])
    b3[y] = s2[...]
    end(c)
    s3[...] = ((b3[0] + b3[1]) + (b3[2] + b3[3])) * scale
    c = swap(3, NZ, at_z, lambda i: s3, b4.at[rows(z, 16)])
    b4[rows(z, 16), :] = s3[...]
    end(c)
    c = swap(4, ND, at_dp, lambda i: b4, s4.at[rows(dp, 128)])
    s4[rows(dp, 128), :] = b4[...]
    end(c)
    out_ref[...] = s4[...]


def total(far, near, scale):
    n = KINDS * 128
    return pl.pallas_call(
        lambda *refs: total_kernel(scale, *refs),
        out_shape=jax.ShapeDtypeStruct((n, 128), F32),
        in_specs=[VM, VM],
        out_specs=VM,
        scratch_shapes=[
            pltpu.VMEM((n, 128), F32),
            pltpu.VMEM((ND, 128, 128), F32),
            pltpu.VMEM((128, 128), F32),
            pltpu.VMEM((NZ, 16, 128), F32),
            pltpu.VMEM((16, 128), F32),
            pltpu.VMEM((NY, 16, 128), F32),
            pltpu.VMEM((16, 128), F32),
            pltpu.VMEM((128, 128), F32),
            pltpu.VMEM((n, 128), F32),
            pltpu.SemaphoreType.DMA((5, 8)),
            pltpu.SemaphoreType.DMA((5, 8)),
        ],
        compiler_params=pltpu.CompilerParams(collective_id=2, has_side_effects=True),
        cost_estimate=cost(33),
        name="total",
    )(far, near)


def unpack_kernel(first_ref, lo_ref, hi_ref, b0, b1, b2, b3, out_ref):
    row = lax.broadcasted_iota(I32, (16, 128), 0)
    y, _ = place()
    for i, back_ref in enumerate((b0, b1, b2, b3)):

        def block(b, c, i=i, back_ref=back_ref):
            d = ((y - i) & (NY - 1)) * NZ + b
            first, lo, hi = first_ref[d], lo_ref[d], hi_ref[d]

            def tile(t, c):
                src = pl.ds(pl.multiple_of(t * 16, 16), 16)
                dst = pl.ds(pl.multiple_of(first + t * 16, 16), 16)
                at = row + t * 16
                new, old = back_ref[b, src, :].astype(F32), out_ref[dst, :].astype(F32)
                out_ref[dst, :] = jnp.where((at >= lo) & (at < hi), new, old).astype(BF16)
                return c

            def plain(t, c):
                src = pl.ds(pl.multiple_of(t * 16, 16), 16)
                out_ref[pl.ds(pl.multiple_of(first + t * 16, 16), 16), :] = back_ref[b, src, :]
                return c

            begin, end = (lo + 15) // 16, hi // 16
            lax.fori_loop(begin, end, plain, 0)
            lax.fori_loop(lo // 16, jnp.minimum(lo // 16 + 1, (hi + 15) // 16), tile, 0)
            lax.fori_loop(jnp.maximum(end, lo // 16 + 1), (hi + 15) // 16, tile, 0)
            return c

        lax.fori_loop(0, NZ, block, 0)


def unpack(first, lo, hi, back, rows):
    return pl.pallas_call(
        unpack_kernel,
        out_shape=jax.ShapeDtypeStruct((rows, 128), BF16),
        in_specs=[SM] * 3 + [VM] * NY,
        out_specs=VM,
        compiler_params=pltpu.CompilerParams(vmem_limit_bytes=VLIM),
        cost_estimate=cost(8),
        name="unpack",
    )(first, lo, hi, *back)


def per_device(features, child_parent, child_code, weight, out_grad):
    feats, cotangent = features[0], out_grad[0]
    fine_rows = feats.shape[0]
    as2d = lambda v: v.reshape(fine_rows // 128, 128)
    blocks, slots, rows, first, lo, hi = pack(as2d(child_parent[0]), as2d(child_code[0]), feats)
    table, want, got, parts = exchange(cotangent, rows, slots, blocks)

    def along_z(v, s):
        if s == 0:
            return v
        return lax.ppermute(v, "space", [(d, d // NZ * NZ + (d + s) % NZ) for d in range(NS)])

    def along_y(v, i):
        if i == 0:
            return v
        return lax.ppermute(v, "space", [(d, (d + i * NZ) % NS) for d in range(NS)])

    arrived = [along_z(v, s) for s, v in enumerate(parts)]
    table = table.reshape(NZ * PAR, 128)
    far, far_term = proxy((2, 1), want, table, weight, parts)
    near, near_term = proxy((3, 0), want, table, weight, parts)
    reply = {**far, **near}
    back = [along_y(reply[i], i) for i in range(NY)]
    grad_rows = fine_rows * NS * lax.axis_size("dp")
    weight_grad = total(far_term, near_term, float(1.0 / grad_rows**0.5))
    first, weight_grad = lax.optimization_barrier((first, weight_grad))
    feature_grad = unpack(first, lo, hi, back, fine_rows)
    got, feature_grad = lax.optimization_barrier((got, feature_grad))
    result = owner(got, weight.reshape(KINDS * 128, 128), arrived)
    return result[None], feature_grad[None], weight_grad.reshape(KINDS, 128, 128)


def solution(mesh):
    placed = (P("dp", "space", None), P("dp", "space"), P("dp", "space"), P(), P("dp", "space", None))
    return jax.shard_map(
        per_device,
        mesh=mesh,
        in_specs=placed,
        out_specs=(P("dp", "space", None), P("dp", "space", None), P()),
        check_vma=False,
    )
```

```python
import jax
import jax.numpy as jnp
from jax import lax
from jax.experimental import pallas as pl
from jax.experimental.pallas import tpu as pltpu
from jax.sharding import PartitionSpec as P


MESH = pl.DeviceIdType.MESH
NY = 4
NZ = 8
NS = NY * NZ
ND = 8
CAP = 528
KINDS = 8
PAR = 2048
SLOTS = KINDS * PAR
F32 = jnp.float32
BF16 = jnp.bfloat16
I32 = jnp.int32
ANY = pl.BlockSpec(memory_space=pl.ANY)
VM = pl.BlockSpec(memory_space=pltpu.VMEM)
SM = pl.BlockSpec(memory_space=pltpu.SMEM)
VLIM = 60 * 1024 * 1024


def cost(us):
    return pl.CostEstimate(flops=0, bytes_accessed=int(us * 3.6e6), transcendentals=0)


def pack_kernel(parent_ref, code_ref, feat_ref, blk_ref, slots_ref, rows_ref, first_ref, lo_ref, hi_ref, par, kind):
    step = pl.program_id(0)
    n = feat_ref.shape[0]

    @pl.when(step == 0)
    def _():
        whole = parent_ref[...]
        par[0 : n // 128, :] = whole
        kind[0 : n // 128, :] = code_ref[...]
        begin = jnp.int32(0)
        for d in range(NS):
            below = jnp.sum((whole < (d + 1) * PAR).astype(F32), axis=0, keepdims=True)
            end = jnp.sum(below).astype(I32)
            first = jnp.minimum(begin // 16 * 16, n - CAP)
            first_ref[d] = first
            lo_ref[d] = begin - first
            hi_ref[d] = end - first
            begin = end

    lane = lax.broadcasted_iota(I32, (8, 128), 1)
    pos = lax.broadcasted_iota(I32, (8, 128), 0) * 128 + lane

    def block(b, c):
        d = step * NZ + b
        first = pl.multiple_of(first_ref[d], 16)
        lo, hi = lo_ref[d], hi_ref[d]
        blk_ref[b] = feat_ref[pl.ds(first, CAP), :]
        at, lane0 = first // 128, lax.rem(first, 128)
        turn = lax.rem(128 - lane0, 128)
        live = (pos >= lo) & (pos < hi)

        def moved(ref):
            here = pltpu.roll(ref[pl.ds(at, 8), :], turn, 1)
            after = pltpu.roll(ref[pl.ds(at + 1, 8), :], turn, 1)
            return jnp.where(lane < 128 - lane0, here, after)

        parents, kinds = moved(par), moved(kind)

        def marked(v, other):
            v = jnp.where(live, v, other)
            return jnp.where(pos == 1022, lo, jnp.where(pos == 1023, hi, v))

        slots_ref[b] = marked(kinds * PAR + (parents & (PAR - 1)), SLOTS)
        rows_ref[b] = marked((parents & (NZ * PAR - 1)) + kinds * (NZ * PAR), SLOTS * NZ)
        return c

    lax.fori_loop(0, NZ, block, 0)


def pack(parents, codes, feats):
    rows = feats.shape[0]
    whole = lambda a: pl.BlockSpec(a.shape, lambda i: (0, 0))
    return pl.pallas_call(
        pack_kernel,
        out_shape=(
            jax.ShapeDtypeStruct((NS, CAP, 128), BF16),
            jax.ShapeDtypeStruct((NS, 8, 128), I32),
            jax.ShapeDtypeStruct((NS, 8, 128), I32),
        )
        + (jax.ShapeDtypeStruct((NS,), I32),) * 3,
        grid=(NY,),
        in_specs=[whole(parents), whole(codes), whole(feats)],
        out_specs=(
            pl.BlockSpec((NZ, CAP, 128), lambda i: (i, 0, 0)),
            pl.BlockSpec((NZ, 8, 128), lambda i: (i, 0, 0)),
            pl.BlockSpec((NZ, 8, 128), lambda i: (i, 0, 0)),
            SM,
            SM,
            SM,
        ),
        scratch_shapes=[pltpu.VMEM((rows // 128 + 16, 128), I32), pltpu.VMEM((rows // 128 + 16, 128), I32)],
        compiler_params=pltpu.CompilerParams(vmem_limit_bytes=VLIM),
        cost_estimate=cost(8),
        name="pack",
    )(parents, codes, feats)


def exchange_kernel(grad_ref, rows_ref, slots_ref, blk_ref, table_ref, want_ref, got_ref, near_ref, *rest):
    parts, (ss, rs, ys, yr, gs, gr, fs, fr, ns, nr, local) = rest[:NZ], rest[NZ:]
    dp, me = lax.axis_index("dp"), lax.axis_index("space")
    y, z = me // NZ, lax.rem(me, NZ)
    barrier = pltpu.get_barrier_semaphore()

    def greet(i, c):
        pl.semaphore_signal(barrier, inc=1, device_id=(dp, lax.rem(me + i, NS)), device_id_type=MESH)
        return c

    lax.fori_loop(1, NS, greet, 0)
    own = [
        pltpu.make_async_copy(grad_ref, table_ref.at[z], local.at[0]),
        pltpu.make_async_copy(rows_ref.at[pl.ds(y * NZ, NZ)], want_ref.at[pl.ds(y * NZ, NZ)], local.at[1]),
        pltpu.make_async_copy(slots_ref.at[me], got_ref.at[me], local.at[2]),
    ]
    for copy in own:
        copy.start()
    pl.semaphore_wait(barrier, NS - 1)
    half = PAR // 2

    def hop(k, side, sub):
        block = lax.rem(z - k + NZ, NZ) if side == 0 else lax.rem(z + k, NZ)
        to = lax.rem(z + 1, NZ) if side == 0 else lax.rem(z + NZ - 1, NZ)
        part = pl.ds(sub * half, half)
        src = grad_ref.at[part] if k == 0 else table_ref.at[block, part]
        return pltpu.make_async_remote_copy(
            src,
            table_ref.at[block, part],
            ss.at[side, k, sub],
            rs.at[side, k, sub],
            device_id=(dp, y * NZ + to),
            device_id_type=MESH,
        )

    chain = [(k, i) for k in range(4) for i in range(2 if k < 3 else 1)]
    hops = {(k, side, i): hop(k, side, side ^ i) for k, i in chain for side in range(2)}

    def rows_to(i):
        ty = lax.rem(y + i, NY)
        return pltpu.make_async_remote_copy(
            rows_ref.at[pl.ds(ty * NZ, NZ)],
            want_ref.at[pl.ds(y * NZ, NZ)],
            ys.at[i],
            yr.at[i],
            device_id=(dp, ty * NZ + z),
            device_id_type=MESH,
        )

    def block_to(i, r):
        ty = lax.rem(y + i, NY)
        return pltpu.make_async_remote_copy(
            blk_ref.at[ty * NZ + lax.rem(z + r, NZ)],
            parts[r].at[i - 1],
            fs.at[i, r],
            fr.at[i, r],
            device_id=(dp, ty * NZ + z),
            device_id_type=MESH,
        )

    moves = [block_to(i, r) for r in range(NZ) for i in range(1, NY)]

    def straight(r):
        tz = lax.rem(z + r, NZ)
        return pltpu.make_async_remote_copy(
            blk_ref.at[y * NZ + tz],
            near_ref.at[r],
            ns.at[r],
            nr.at[r],
            device_id=(dp, y * NZ + tz),
            device_id_type=MESH,
        )

    straights = [straight(r) for r in (1, 7, 2, 6, 3, 5, 4)]

    def slots_to(i):
        t = lax.rem(me + i, NS)
        return pltpu.make_async_remote_copy(
            slots_ref.at[t], got_ref.at[me], gs.at[i], gr.at[i], device_id=(dp, t), device_id_type=MESH
        )

    for i in range(2):
        for side in range(2):
            hops[0, side, i].start()
    for i in range(1, NY):
        rows_to(i).start()

    def start_slots(i, c):
        slots_to(i).start()
        return c

    lax.fori_loop(1, NS, start_slots, 0)
    for move in moves:
        move.start()
    for k, i in chain:
        if (k, i) == (2, 1):
            for move in straights:
                move.start()
        for side in range(2):
            hops[k, side, i].wait_recv()
            if (k + 1, side, i) in hops:
                hops[k + 1, side, i].start()
    for copy in hops.values():
        copy.wait_send()
    for move in moves + straights:
        move.wait()
    for i in range(1, NY):
        rows_to(i).wait()

    def end_slots(i, c):
        slots_to(i).wait()
        return c

    lax.fori_loop(1, NS, end_slots, 0)
    for copy in own:
        copy.wait()


def exchange(grad, rows, slots, blocks):
    ints = jax.ShapeDtypeStruct((NS, 8, 128), I32)
    part = jax.ShapeDtypeStruct((NY - 1, CAP, 128), BF16)
    near = jax.ShapeDtypeStruct((NZ, CAP, 128), BF16)
    dma = pltpu.SemaphoreType.DMA
    sems = [(2, 4, 2), (2, 4, 2), (NY,), (NY,), (NS,), (NS,), (NY, NZ), (NY, NZ), (NZ,), (NZ,), (3,)]
    out = pl.pallas_call(
        exchange_kernel,
        out_shape=(jax.ShapeDtypeStruct((NZ, PAR, 128), BF16), ints, ints, near) + (part,) * NZ,
        in_specs=[ANY] * 4,
        out_specs=(ANY,) * (4 + NZ),
        scratch_shapes=[dma(n) for n in sems],
        compiler_params=pltpu.CompilerParams(collective_id=1, has_side_effects=True),
        cost_estimate=cost(50),
        name="exchange",
    )(grad, rows, slots, blocks)
    return *out[:4], out[4:]


def place():
    me = lax.axis_index("space")
    return me >> 3, me & (NZ - 1)


def proxy_kernel(distances, want_ref, codes_ref, table_ref, weight_ref, blk_ref, *rest):
    n = len(distances)
    parts, outs = rest[:NZ], rest[NZ : NZ + n]
    term_ref, wide, rowbuf, feats, acc, turned_weight, sems = rest[NZ + n :]
    y, z = place()
    copies = [
        pltpu.make_async_copy(
            part.at[NY - 1 - i] if i else blk_ref.at[y * NZ + ((z + r) & (NZ - 1))], feats.at[r, m], sems.at[r, m]
        )
        for m, i in enumerate(distances)
        for r, part in enumerate(parts)
    ]
    for copy in copies:
        copy.start()
    acc[...] = jnp.zeros(acc.shape, F32)
    for k in range(KINDS):
        turned_weight[k * 128 : (k + 1) * 128, :] = jnp.transpose(weight_ref[k])

    def widen(i, c):
        at = pl.ds(pl.multiple_of(i * 512, 512), 512)
        wide[at, :] = table_ref[at, :].astype(F32)
        return c

    lax.fori_loop(0, NZ * PAR // 512, widen, 0)
    for copy in copies:
        copy.wait()

    for m, out_ref in enumerate(outs):
        q = (y + distances[m]) & (NY - 1)

        def block(r, c, m=m, q=q, out_ref=out_ref):
            zz = (z + r) & (NZ - 1)
            at = q * NZ + zz
            base = at * 1024
            lo, hi = want_ref[base + 1022], want_ref[base + 1023]

            def group(g, c):
                for u in range(16):
                    j = g * 16 + u
                    rowbuf[pl.ds(j, 1), :] = wide[pl.ds(want_ref[base + j] & (NZ * PAR - 1), 1), :]
                return c

            lax.fori_loop(lo // 16, (hi + 15) // 16, group, 0)
            codes = jnp.transpose((codes_ref[at] >> 14).astype(F32))

            def piece(first, last):
                cols = range(first // 128, (last + 127) // 128)
                kinds = [jnp.broadcast_to(codes[: min(128, last - m * 128), m : m + 1], (min(128, last - m * 128), 128)) for m in cols]
                kinds = jnp.concatenate(kinds, axis=0)
                rows = rowbuf[first:last, :]
                none = jnp.zeros(rows.shape, F32)
                placed = [jnp.where(kinds == k, rows, none).astype(BF16) for k in range(KINDS)]
                placed = jnp.concatenate(placed, axis=1)
                grads = jnp.dot(placed, turned_weight[...], preferred_element_type=F32)
                out_ref[zz, first:last, :] = grads.astype(BF16)
                turned = jnp.transpose(feats[r, m, first:last, :])
                acc[...] += jnp.dot(turned, placed, preferred_element_type=F32)

            piece(0, 256)

            @pl.when(hi > 256)
            def _():
                piece(256, CAP)

            return c

        lax.fori_loop(0, NZ, block, 0)
    for k in range(KINDS):
        part = slice(k * 128, (k + 1) * 128)
        term_ref[part, :] = acc[:, part]


def proxy(distances, want, table, weight, blocks, parts):
    n = len(distances)
    *rows, term = pl.pallas_call(
        lambda *refs: proxy_kernel(distances, *refs),
        out_shape=(jax.ShapeDtypeStruct((NZ, CAP, 128), BF16),) * n
        + (jax.ShapeDtypeStruct((KINDS * 128, 128), F32),),
        in_specs=[SM, VM, VM, VM] + [ANY] * (NZ + 1),
        out_specs=(VM,) * (n + 1),
        scratch_shapes=[
            pltpu.VMEM((NZ * PAR, 128), F32),
            pltpu.VMEM((CAP, 128), F32),
            pltpu.VMEM((NZ, n, CAP, 128), BF16),
            pltpu.VMEM((128, KINDS * 128), F32),
            pltpu.VMEM((KINDS * 128, 128), BF16),
            pltpu.SemaphoreType.DMA((NZ, n)),
        ],
        compiler_params=pltpu.CompilerParams(vmem_limit_bytes=VLIM),
        cost_estimate=cost(20),
        name="proxy",
    )(want.reshape(-1), want, table, weight, blocks, *parts)
    return dict(zip(distances, rows)), term


def owner_kernel(slot_ref, weight_ref, blk_ref, near_ref, *rest):
    parts = rest[:NZ]
    out_ref, grid_ref, rowbuf, feats, sems = rest[NZ:]
    y, z = place()
    copies = [
        (
            pltpu.make_async_copy(part, feats.at[s, pl.ds(1, NY - 1)], sems.at[s, 0]),
            pltpu.make_async_copy(near_ref.at[s] if s else blk_ref.at[y * NZ + z], feats.at[s, 0], sems.at[s, 1]),
        )
        for s, part in enumerate(parts)
    ]
    for pair in copies:
        for copy in pair:
            copy.start()

    def clear(i, c):
        grid_ref[pl.ds(pl.multiple_of(i * 512, 512), 512), :] = jnp.zeros((512, 128), F32)
        return c

    lax.fori_loop(0, SLOTS // 512, clear, 0)

    for s in range(NZ):
        for copy in copies[s]:
            copy.wait()

        def block(i, c, s=s):
            base = (((y - i) & (NY - 1)) * NZ + ((z - s) & (NZ - 1))) * 1024
            lo, hi = slot_ref[base + 1022], slot_ref[base + 1023]
            rowbuf[...] = feats[s, i].astype(F32)

            def group(g, c):
                for u in range(16):
                    j = g * 16 + u
                    grid_ref[pl.ds(slot_ref[base + j], 1), :] = rowbuf[pl.ds(j, 1), :]
                return c

            lax.fori_loop(lo // 16, (hi + 15) // 16, group, 0)
            return c

        lax.fori_loop(0, NY, block, 0)

    def chunk(i, c):
        total = jnp.zeros((512, 128), F32)
        for k in range(0, KINDS, 2):
            pair = [grid_ref[pl.ds(pl.multiple_of(m * PAR + i * 512, 512), 512), :].astype(BF16) for m in (k, k + 1)]
            kids = jnp.concatenate(pair, axis=1)
            total = total + jnp.dot(kids, weight_ref[k * 128 : (k + 2) * 128, :], preferred_element_type=F32)
        out_ref[pl.ds(pl.multiple_of(i * 512, 512), 512), :] = total.astype(BF16)
        return c

    lax.fori_loop(0, PAR // 512, chunk, 0)


def owner(slots, weight, blocks, near, parts):
    return pl.pallas_call(
        owner_kernel,
        out_shape=jax.ShapeDtypeStruct((PAR, 128), BF16),
        in_specs=[SM, VM] + [ANY] * (NZ + 2),
        out_specs=VM,
        scratch_shapes=[
            pltpu.VMEM((SLOTS + 8, 128), F32),
            pltpu.VMEM((CAP, 128), F32),
            pltpu.VMEM((NZ, NY, CAP, 128), BF16),
            pltpu.SemaphoreType.DMA((NZ, 2)),
        ],
        compiler_params=pltpu.CompilerParams(vmem_limit_bytes=VLIM),
        cost_estimate=cost(18),
        name="owner",
    )(slots.reshape(-1), weight, blocks, near, *parts)


def total_kernel(scale, far_ref, near_ref, out_ref, term_ref, b1, s1, b2, s2, b3, s3, b4, s4, send, recv):
    dp, me = lax.axis_index("dp"), lax.axis_index("space")
    y, z = me // NZ, lax.rem(me, NZ)
    at_dp = lambda i: (lax.rem(dp + i, ND), me)
    at_z = lambda i: (dp, y * NZ + lax.rem(z + i, NZ))
    at_y = lambda i: (dp, lax.rem(y + i, NY) * NZ + z)
    term_ref[...] = far_ref[...] + near_ref[...]
    barrier = pltpu.get_barrier_semaphore()
    for who, n in ((at_dp, ND), (at_z, NZ), (at_y, NY)):
        for i in range(1, n):
            pl.semaphore_signal(barrier, inc=1, device_id=who(i), device_id_type=MESH)
    pl.semaphore_wait(barrier, ND + NZ + NY - 3)

    def swap(phase, n, who, src, dst):
        copies = [
            pltpu.make_async_remote_copy(
                src(i), dst, send.at[phase, i], recv.at[phase, i], device_id=who(i), device_id_type=MESH
            )
            for i in range(1, n)
        ]
        for c in copies:
            c.start()
        return copies

    def end(copies):
        for c in copies:
            c.wait()

    def rows(i, n):
        return pl.ds(pl.multiple_of(i * n, n), n)

    c = swap(0, ND, at_dp, lambda i: term_ref.at[rows(lax.rem(dp + i, ND), 128)], b1.at[dp])
    b1[dp] = term_ref[rows(dp, 128), :]
    end(c)
    s1[...] = ((b1[0] + b1[1]) + (b1[2] + b1[3])) + ((b1[4] + b1[5]) + (b1[6] + b1[7]))
    c = swap(1, NZ, at_z, lambda i: s1.at[rows(lax.rem(z + i, NZ), 16)], b2.at[z])
    b2[z] = s1[rows(z, 16), :]
    end(c)
    s2[...] = ((b2[0] + b2[1]) + (b2[2] + b2[3])) + ((b2[4] + b2[5]) + (b2[6] + b2[7]))
    c = swap(2, NY, at_y, lambda i: s2, b3.at[y])
    b3[y] = s2[...]
    end(c)
    s3[...] = ((b3[0] + b3[1]) + (b3[2] + b3[3])) * scale
    c = swap(3, NZ, at_z, lambda i: s3, b4.at[rows(z, 16)])
    b4[rows(z, 16), :] = s3[...]
    end(c)
    c = swap(4, ND, at_dp, lambda i: b4, s4.at[rows(dp, 128)])
    s4[rows(dp, 128), :] = b4[...]
    end(c)
    out_ref[...] = s4[...]


def total(far, near, scale):
    n = KINDS * 128
    return pl.pallas_call(
        lambda *refs: total_kernel(scale, *refs),
        out_shape=jax.ShapeDtypeStruct((n, 128), F32),
        in_specs=[VM, VM],
        out_specs=VM,
        scratch_shapes=[
            pltpu.VMEM((n, 128), F32),
            pltpu.VMEM((ND, 128, 128), F32),
            pltpu.VMEM((128, 128), F32),
            pltpu.VMEM((NZ, 16, 128), F32),
            pltpu.VMEM((16, 128), F32),
            pltpu.VMEM((NY, 16, 128), F32),
            pltpu.VMEM((16, 128), F32),
            pltpu.VMEM((128, 128), F32),
            pltpu.VMEM((n, 128), F32),
            pltpu.SemaphoreType.DMA((5, 8)),
            pltpu.SemaphoreType.DMA((5, 8)),
        ],
        compiler_params=pltpu.CompilerParams(collective_id=2, has_side_effects=True),
        cost_estimate=cost(33),
        name="total",
    )(far, near)


def unpack_kernel(first_ref, lo_ref, hi_ref, b0, b1, b2, b3, out_ref):
    row = lax.broadcasted_iota(I32, (16, 128), 0)
    y, _ = place()
    for i, back_ref in enumerate((b0, b1, b2, b3)):

        def block(b, c, i=i, back_ref=back_ref):
            d = ((y - i) & (NY - 1)) * NZ + b
            first, lo, hi = first_ref[d], lo_ref[d], hi_ref[d]

            def tile(t, c):
                src = pl.ds(pl.multiple_of(t * 16, 16), 16)
                dst = pl.ds(pl.multiple_of(first + t * 16, 16), 16)
                at = row + t * 16
                new, old = back_ref[b, src, :].astype(F32), out_ref[dst, :].astype(F32)
                out_ref[dst, :] = jnp.where((at >= lo) & (at < hi), new, old).astype(BF16)
                return c

            def plain(t, c):
                src = pl.ds(pl.multiple_of(t * 16, 16), 16)
                out_ref[pl.ds(pl.multiple_of(first + t * 16, 16), 16), :] = back_ref[b, src, :]
                return c

            begin, end = (lo + 15) // 16, hi // 16
            lax.fori_loop(begin, end, plain, 0)
            lax.fori_loop(lo // 16, jnp.minimum(lo // 16 + 1, (hi + 15) // 16), tile, 0)
            lax.fori_loop(jnp.maximum(end, lo // 16 + 1), (hi + 15) // 16, tile, 0)
            return c

        lax.fori_loop(0, NZ, block, 0)


def unpack(first, lo, hi, back, rows):
    return pl.pallas_call(
        unpack_kernel,
        out_shape=jax.ShapeDtypeStruct((rows, 128), BF16),
        in_specs=[SM] * 3 + [VM] * NY,
        out_specs=VM,
        compiler_params=pltpu.CompilerParams(vmem_limit_bytes=VLIM),
        cost_estimate=cost(8),
        name="unpack",
    )(first, lo, hi, *back)


def per_device(features, child_parent, child_code, weight, out_grad):
    feats, cotangent = features[0], out_grad[0]
    fine_rows = feats.shape[0]
    as2d = lambda v: v.reshape(fine_rows // 128, 128)
    blocks, slots, rows, first, lo, hi = pack(as2d(child_parent[0]), as2d(child_code[0]), feats)
    table, want, got, near_blocks, parts = exchange(cotangent, rows, slots, blocks)

    def along_z(v, s):
        if s == 0:
            return v
        return lax.ppermute(v, "space", [(d, d // NZ * NZ + (d + s) % NZ) for d in range(NS)])

    def along_y(v, i):
        if i == 0:
            return v
        return lax.ppermute(v, "space", [(d, (d + i * NZ) % NS) for d in range(NS)])

    arrived = [along_z(v, s) for s, v in enumerate(parts)]
    table = table.reshape(NZ * PAR, 128)
    far, far_term = proxy((2, 1), want, table, weight, blocks, parts)
    near, near_term = proxy((3, 0), want, table, weight, blocks, parts)
    reply = {**far, **near}
    back = [along_y(reply[i], i) for i in range(NY)]
    grad_rows = fine_rows * NS * lax.axis_size("dp")
    weight_grad = total(far_term, near_term, float(1.0 / grad_rows**0.5))
    first, weight_grad = lax.optimization_barrier((first, weight_grad))
    feature_grad = unpack(first, lo, hi, back, fine_rows)
    got, feature_grad = lax.optimization_barrier((got, feature_grad))
    result = owner(got, weight.reshape(KINDS * 128, 128), blocks, near_blocks, arrived)
    return result[None], feature_grad[None], weight_grad.reshape(KINDS, 128, 128)


def solution(mesh):
    placed = (P("dp", "space", None), P("dp", "space"), P("dp", "space"), P(), P("dp", "space", None))
    return jax.shard_map(
        per_device,
        mesh=mesh,
        in_specs=placed,
        out_specs=(P("dp", "space", None), P("dp", "space", None), P()),
        check_vma=False,
    )
```

```python
import jax
import jax.numpy as jnp
from jax import lax
from jax.experimental import pallas as pl
from jax.experimental.pallas import tpu as pltpu
from jax.sharding import PartitionSpec as P


MESH = pl.DeviceIdType.MESH
NY = 4
NZ = 8
NS = NY * NZ
ND = 8
CAP = 528
KINDS = 8
PAR = 2048
SLOTS = KINDS * PAR
F32 = jnp.float32
BF16 = jnp.bfloat16
I32 = jnp.int32
ANY = pl.BlockSpec(memory_space=pl.ANY)
VM = pl.BlockSpec(memory_space=pltpu.VMEM)
SM = pl.BlockSpec(memory_space=pltpu.SMEM)
VLIM = 60 * 1024 * 1024


def cost(us):
    return pl.CostEstimate(flops=0, bytes_accessed=int(us * 3.6e6), transcendentals=0)


def pack_kernel(parent_ref, code_ref, feat_ref, blk_ref, slots_ref, rows_ref, first_ref, lo_ref, hi_ref, par, kind):
    step = pl.program_id(0)
    n = feat_ref.shape[0]

    @pl.when(step == 0)
    def _():
        whole = parent_ref[...]
        par[0 : n // 128, :] = whole
        kind[0 : n // 128, :] = code_ref[...]
        begin = jnp.int32(0)
        for d in range(NS):
            below = jnp.sum((whole < (d + 1) * PAR).astype(F32), axis=0, keepdims=True)
            end = jnp.sum(below).astype(I32)
            first = jnp.minimum(begin // 16 * 16, n - CAP)
            first_ref[d] = first
            lo_ref[d] = begin - first
            hi_ref[d] = end - first
            begin = end

    lane = lax.broadcasted_iota(I32, (8, 128), 1)
    pos = lax.broadcasted_iota(I32, (8, 128), 0) * 128 + lane

    def block(b, c):
        d = step * NZ + b
        first = pl.multiple_of(first_ref[d], 16)
        lo, hi = lo_ref[d], hi_ref[d]
        blk_ref[b] = feat_ref[pl.ds(first, CAP), :]
        at, lane0 = first // 128, lax.rem(first, 128)
        turn = lax.rem(128 - lane0, 128)
        live = (pos >= lo) & (pos < hi)

        def moved(ref):
            here = pltpu.roll(ref[pl.ds(at, 8), :], turn, 1)
            after = pltpu.roll(ref[pl.ds(at + 1, 8), :], turn, 1)
            return jnp.where(lane < 128 - lane0, here, after)

        parents, kinds = moved(par), moved(kind)

        def marked(v, other):
            v = jnp.where(live, v, other)
            return jnp.where(pos == 1022, lo, jnp.where(pos == 1023, hi, v))

        slots_ref[b] = marked(kinds * PAR + (parents & (PAR - 1)), SLOTS)
        rows_ref[b] = marked((parents & (NZ * PAR - 1)) + kinds * (NZ * PAR), SLOTS * NZ)
        return c

    lax.fori_loop(0, NZ, block, 0)


def pack(parents, codes, feats):
    rows = feats.shape[0]
    whole = lambda a: pl.BlockSpec(a.shape, lambda i: (0, 0))
    return pl.pallas_call(
        pack_kernel,
        out_shape=(
            jax.ShapeDtypeStruct((NS, CAP, 128), BF16),
            jax.ShapeDtypeStruct((NS, 8, 128), I32),
            jax.ShapeDtypeStruct((NS, 8, 128), I32),
        )
        + (jax.ShapeDtypeStruct((NS,), I32),) * 3,
        grid=(NY,),
        in_specs=[whole(parents), whole(codes), whole(feats)],
        out_specs=(
            pl.BlockSpec((NZ, CAP, 128), lambda i: (i, 0, 0)),
            pl.BlockSpec((NZ, 8, 128), lambda i: (i, 0, 0)),
            pl.BlockSpec((NZ, 8, 128), lambda i: (i, 0, 0)),
            SM,
            SM,
            SM,
        ),
        scratch_shapes=[pltpu.VMEM((rows // 128 + 16, 128), I32), pltpu.VMEM((rows // 128 + 16, 128), I32)],
        compiler_params=pltpu.CompilerParams(vmem_limit_bytes=VLIM),
        cost_estimate=cost(8),
        name="pack",
    )(parents, codes, feats)


def exchange_kernel(grad_ref, rows_ref, slots_ref, blk_ref, table_ref, want_ref, got_ref, near_ref, *rest):
    parts, (ss, rs, ys, yr, gs, gr, fs, fr, ns, nr, local) = rest[:NZ], rest[NZ:]
    dp, me = lax.axis_index("dp"), lax.axis_index("space")
    y, z = me // NZ, lax.rem(me, NZ)
    barrier = pltpu.get_barrier_semaphore()

    def greet(i, c):
        pl.semaphore_signal(barrier, inc=1, device_id=(dp, lax.rem(me + i, NS)), device_id_type=MESH)
        return c

    lax.fori_loop(1, NS, greet, 0)
    own = [
        pltpu.make_async_copy(grad_ref, table_ref.at[z], local.at[0]),
        pltpu.make_async_copy(rows_ref.at[pl.ds(y * NZ, NZ)], want_ref.at[pl.ds(y * NZ, NZ)], local.at[1]),
        pltpu.make_async_copy(slots_ref.at[me], got_ref.at[me], local.at[2]),
    ]
    for copy in own:
        copy.start()
    pl.semaphore_wait(barrier, NS - 1)
    half = PAR // 2

    def hop(k, side, sub):
        block = lax.rem(z - k + NZ, NZ) if side == 0 else lax.rem(z + k, NZ)
        to = lax.rem(z + 1, NZ) if side == 0 else lax.rem(z + NZ - 1, NZ)
        part = pl.ds(sub * half, half)
        src = grad_ref.at[part] if k == 0 else table_ref.at[block, part]
        return pltpu.make_async_remote_copy(
            src,
            table_ref.at[block, part],
            ss.at[side, k, sub],
            rs.at[side, k, sub],
            device_id=(dp, y * NZ + to),
            device_id_type=MESH,
        )

    chain = [(k, i) for k in range(4) for i in range(2 if k < 3 else 1)]
    hops = {(k, side, i): hop(k, side, side ^ i) for k, i in chain for side in range(2)}

    def rows_to(i):
        ty = lax.rem(y + i, NY)
        return pltpu.make_async_remote_copy(
            rows_ref.at[pl.ds(ty * NZ, NZ)],
            want_ref.at[pl.ds(y * NZ, NZ)],
            ys.at[i],
            yr.at[i],
            device_id=(dp, ty * NZ + z),
            device_id_type=MESH,
        )

    def block_to(i, r):
        ty = lax.rem(y + i, NY)
        return pltpu.make_async_remote_copy(
            blk_ref.at[ty * NZ + lax.rem(z + r, NZ)],
            parts[r].at[i - 1],
            fs.at[i, r],
            fr.at[i, r],
            device_id=(dp, ty * NZ + z),
            device_id_type=MESH,
        )

    moves = [block_to(i, r) for r in range(NZ) for i in range(1, NY)]

    def straight(r):
        tz = lax.rem(z + r, NZ)
        return pltpu.make_async_remote_copy(
            blk_ref.at[y * NZ + tz],
            near_ref.at[r],
            ns.at[r],
            nr.at[r],
            device_id=(dp, y * NZ + tz),
            device_id_type=MESH,
        )

    straights = [straight(r) for r in (1, 7, 2, 6, 3, 5, 4)]

    def slots_to(i):
        t = lax.rem(me + i, NS)
        return pltpu.make_async_remote_copy(
            slots_ref.at[t], got_ref.at[me], gs.at[i], gr.at[i], device_id=(dp, t), device_id_type=MESH
        )

    for i in range(2):
        for side in range(2):
            hops[0, side, i].start()
    for i in range(1, NY):
        rows_to(i).start()

    def start_slots(i, c):
        slots_to(i).start()
        return c

    lax.fori_loop(1, NS, start_slots, 0)
    for move in moves:
        move.start()
    for k, i in chain:
        if (k, i) == (2, 1):
            for move in straights:
                move.start()
        for side in range(2):
            hops[k, side, i].wait_recv()
            if (k + 1, side, i) in hops:
                hops[k + 1, side, i].start()
    for copy in hops.values():
        copy.wait_send()
    for move in moves + straights:
        move.wait()
    for i in range(1, NY):
        rows_to(i).wait()

    def end_slots(i, c):
        slots_to(i).wait()
        return c

    lax.fori_loop(1, NS, end_slots, 0)
    for copy in own:
        copy.wait()


def exchange(grad, rows, slots, blocks):
    ints = jax.ShapeDtypeStruct((NS, 8, 128), I32)
    part = jax.ShapeDtypeStruct((NY - 1, CAP, 128), BF16)
    near = jax.ShapeDtypeStruct((NZ, CAP, 128), BF16)
    dma = pltpu.SemaphoreType.DMA
    sems = [(2, 4, 2), (2, 4, 2), (NY,), (NY,), (NS,), (NS,), (NY, NZ), (NY, NZ), (NZ,), (NZ,), (3,)]
    out = pl.pallas_call(
        exchange_kernel,
        out_shape=(jax.ShapeDtypeStruct((NZ, PAR, 128), BF16), ints, ints, near) + (part,) * NZ,
        in_specs=[ANY] * 4,
        out_specs=(ANY,) * (4 + NZ),
        scratch_shapes=[dma(n) for n in sems],
        compiler_params=pltpu.CompilerParams(collective_id=1, has_side_effects=True),
        cost_estimate=cost(50),
        name="exchange",
    )(grad, rows, slots, blocks)
    return *out[:4], out[4:]


def place():
    me = lax.axis_index("space")
    return me >> 3, me & (NZ - 1)


def proxy_kernel(distances, want_ref, codes_ref, table_ref, weight_ref, blk_ref, *rest):
    n = len(distances)
    parts, outs = rest[:NZ], rest[NZ : NZ + n]
    term_ref, wide, rowbuf, feats, acc, turned_weight, sems = rest[NZ + n :]
    y, z = place()
    copies = [
        pltpu.make_async_copy(
            part.at[NY - 1 - i] if i else blk_ref.at[y * NZ + ((z + r) & (NZ - 1))], feats.at[r, m], sems.at[r, m]
        )
        for m, i in enumerate(distances)
        for r, part in enumerate(parts)
    ]
    for copy in copies:
        copy.start()
    acc[...] = jnp.zeros(acc.shape, F32)
    for k in range(KINDS):
        half, kk = k // 4, k % 4
        turned_weight[kk * 128 : (kk + 1) * 128, half * 128 : (half + 1) * 128] = jnp.transpose(weight_ref[k])

    def widen(i, c):
        at = pl.ds(pl.multiple_of(i * 512, 512), 512)
        wide[at, :] = table_ref[at, :].astype(F32)
        return c

    lax.fori_loop(0, NZ * PAR // 512, widen, 0)
    for copy in copies:
        copy.wait()

    for m, out_ref in enumerate(outs):
        q = (y + distances[m]) & (NY - 1)

        def block(r, c, m_at=m, q=q, out_ref=out_ref):
            zz = (z + r) & (NZ - 1)
            at = q * NZ + zz
            base = at * 1024
            lo, hi = want_ref[base + 1022], want_ref[base + 1023]

            def group(g, c):
                for u in range(16):
                    j = g * 16 + u
                    rowbuf[pl.ds(j, 1), :] = wide[pl.ds(want_ref[base + j] & (NZ * PAR - 1), 1), :]
                return c

            lax.fori_loop(lo // 16, (hi + 15) // 16, group, 0)
            codes = (codes_ref[at] >> 14).astype(F32)
            columns = jnp.transpose(codes)

            def piece(first, last):
                n = last - first
                cols = range(first // 128, (last + 127) // 128)
                tall = [min(128, last - m * 128) for m in cols]
                kinds = [jnp.broadcast_to(columns[:t, m : m + 1], (t, 128)) for m, t in zip(cols, tall)]
                kinds = jnp.concatenate(kinds, axis=0)
                upper = kinds >= 4.0
                quarter = jnp.where(upper, kinds - 4.0, kinds)
                rows = rowbuf[first:last, :]
                none = jnp.zeros(rows.shape, F32)
                placed = [jnp.where(quarter == kk, rows, none).astype(BF16) for kk in range(4)]
                placed = jnp.concatenate(placed, axis=1)
                both = jnp.dot(placed, turned_weight[...], preferred_element_type=F32)
                out_ref[zz, first:last, :] = jnp.where(upper, both[:, 128:], both[:, :128]).astype(BF16)
                turned = jnp.transpose(feats[r, m_at, first:last, :]).astype(F32)
                across = jnp.concatenate([codes[m : m + 1, :] for m in cols], axis=1)[:, :n]
                upper = jnp.broadcast_to(across, (128, n)) >= 4.0
                none = jnp.zeros((128, n), F32)
                split = [jnp.where(upper, none, turned).astype(BF16), jnp.where(upper, turned, none).astype(BF16)]
                acc[...] += jnp.dot(jnp.concatenate(split, axis=0), placed, preferred_element_type=F32)

            piece(0, 256)

            @pl.when(hi > 256)
            def _():
                piece(256, CAP)

            return c

        lax.fori_loop(0, NZ, block, 0)
    for k in range(KINDS):
        half, kk = k // 4, k % 4
        term_ref[k * 128 : (k + 1) * 128, :] = acc[half * 128 : (half + 1) * 128, kk * 128 : (kk + 1) * 128]


def proxy(distances, want, table, weight, blocks, parts):
    n = len(distances)
    *rows, term = pl.pallas_call(
        lambda *refs: proxy_kernel(distances, *refs),
        out_shape=(jax.ShapeDtypeStruct((NZ, CAP, 128), BF16),) * n
        + (jax.ShapeDtypeStruct((KINDS * 128, 128), F32),),
        in_specs=[SM, VM, VM, VM] + [ANY] * (NZ + 1),
        out_specs=(VM,) * (n + 1),
        scratch_shapes=[
            pltpu.VMEM((NZ * PAR, 128), F32),
            pltpu.VMEM((CAP, 128), F32),
            pltpu.VMEM((NZ, n, CAP, 128), BF16),
            pltpu.VMEM((256, 512), F32),
            pltpu.VMEM((512, 256), BF16),
            pltpu.SemaphoreType.DMA((NZ, n)),
        ],
        compiler_params=pltpu.CompilerParams(vmem_limit_bytes=VLIM),
        cost_estimate=cost(20),
        name="proxy",
    )(want.reshape(-1), want, table, weight, blocks, *parts)
    return dict(zip(distances, rows)), term


def owner_kernel(slot_ref, weight_ref, blk_ref, near_ref, *rest):
    parts = rest[:NZ]
    out_ref, grid_ref, rowbuf, feats, sems = rest[NZ:]
    y, z = place()
    copies = [
        (
            pltpu.make_async_copy(part, feats.at[s, pl.ds(1, NY - 1)], sems.at[s, 0]),
            pltpu.make_async_copy(near_ref.at[s] if s else blk_ref.at[y * NZ + z], feats.at[s, 0], sems.at[s, 1]),
        )
        for s, part in enumerate(parts)
    ]
    for pair in copies:
        for copy in pair:
            copy.start()

    def clear(i, c):
        grid_ref[pl.ds(pl.multiple_of(i * 512, 512), 512), :] = jnp.zeros((512, 128), F32)
        return c

    lax.fori_loop(0, SLOTS // 512, clear, 0)

    for s in range(NZ):
        for copy in copies[s]:
            copy.wait()

        def block(i, c, s=s):
            base = (((y - i) & (NY - 1)) * NZ + ((z - s) & (NZ - 1))) * 1024
            lo, hi = slot_ref[base + 1022], slot_ref[base + 1023]
            rowbuf[...] = feats[s, i].astype(F32)

            def group(g, c):
                for u in range(16):
                    j = g * 16 + u
                    grid_ref[pl.ds(slot_ref[base + j], 1), :] = rowbuf[pl.ds(j, 1), :]
                return c

            lax.fori_loop(lo // 16, (hi + 15) // 16, group, 0)
            return c

        lax.fori_loop(0, NY, block, 0)

    def chunk(i, c):
        total = jnp.zeros((512, 128), F32)
        for k in range(0, KINDS, 2):
            pair = [grid_ref[pl.ds(pl.multiple_of(m * PAR + i * 512, 512), 512), :].astype(BF16) for m in (k, k + 1)]
            kids = jnp.concatenate(pair, axis=1)
            total = total + jnp.dot(kids, weight_ref[k * 128 : (k + 2) * 128, :], preferred_element_type=F32)
        out_ref[pl.ds(pl.multiple_of(i * 512, 512), 512), :] = total.astype(BF16)
        return c

    lax.fori_loop(0, PAR // 512, chunk, 0)


def owner(slots, weight, blocks, near, parts):
    return pl.pallas_call(
        owner_kernel,
        out_shape=jax.ShapeDtypeStruct((PAR, 128), BF16),
        in_specs=[SM, VM] + [ANY] * (NZ + 2),
        out_specs=VM,
        scratch_shapes=[
            pltpu.VMEM((SLOTS + 8, 128), F32),
            pltpu.VMEM((CAP, 128), F32),
            pltpu.VMEM((NZ, NY, CAP, 128), BF16),
            pltpu.SemaphoreType.DMA((NZ, 2)),
        ],
        compiler_params=pltpu.CompilerParams(vmem_limit_bytes=VLIM),
        cost_estimate=cost(18),
        name="owner",
    )(slots.reshape(-1), weight, blocks, near, *parts)


def total_kernel(scale, far_ref, near_ref, out_ref, term_ref, b1, s1, b2, s2, b3, s3, b4, s4, send, recv):
    dp, me = lax.axis_index("dp"), lax.axis_index("space")
    y, z = me // NZ, lax.rem(me, NZ)
    at_dp = lambda i: (lax.rem(dp + i, ND), me)
    at_z = lambda i: (dp, y * NZ + lax.rem(z + i, NZ))
    at_y = lambda i: (dp, lax.rem(y + i, NY) * NZ + z)
    term_ref[...] = far_ref[...] + near_ref[...]
    barrier = pltpu.get_barrier_semaphore()
    for who, n in ((at_dp, ND), (at_z, NZ), (at_y, NY)):
        for i in range(1, n):
            pl.semaphore_signal(barrier, inc=1, device_id=who(i), device_id_type=MESH)
    pl.semaphore_wait(barrier, ND + NZ + NY - 3)

    def swap(phase, n, who, src, dst):
        copies = [
            pltpu.make_async_remote_copy(
                src(i), dst, send.at[phase, i], recv.at[phase, i], device_id=who(i), device_id_type=MESH
            )
            for i in range(1, n)
        ]
        for c in copies:
            c.start()
        return copies

    def end(copies):
        for c in copies:
            c.wait()

    def rows(i, n):
        return pl.ds(pl.multiple_of(i * n, n), n)

    c = swap(0, ND, at_dp, lambda i: term_ref.at[rows(lax.rem(dp + i, ND), 128)], b1.at[dp])
    b1[dp] = term_ref[rows(dp, 128), :]
    end(c)
    s1[...] = ((b1[0] + b1[1]) + (b1[2] + b1[3])) + ((b1[4] + b1[5]) + (b1[6] + b1[7]))
    c = swap(1, NZ, at_z, lambda i: s1.at[rows(lax.rem(z + i, NZ), 16)], b2.at[z])
    b2[z] = s1[rows(z, 16), :]
    end(c)
    s2[...] = ((b2[0] + b2[1]) + (b2[2] + b2[3])) + ((b2[4] + b2[5]) + (b2[6] + b2[7]))
    c = swap(2, NY, at_y, lambda i: s2, b3.at[y])
    b3[y] = s2[...]
    end(c)
    s3[...] = ((b3[0] + b3[1]) + (b3[2] + b3[3])) * scale
    c = swap(3, NZ, at_z, lambda i: s3, b4.at[rows(z, 16)])
    b4[rows(z, 16), :] = s3[...]
    end(c)
    c = swap(4, ND, at_dp, lambda i: b4, s4.at[rows(dp, 128)])
    s4[rows(dp, 128), :] = b4[...]
    end(c)
    out_ref[...] = s4[...]


def total(far, near, scale):
    n = KINDS * 128
    return pl.pallas_call(
        lambda *refs: total_kernel(scale, *refs),
        out_shape=jax.ShapeDtypeStruct((n, 128), F32),
        in_specs=[VM, VM],
        out_specs=VM,
        scratch_shapes=[
            pltpu.VMEM((n, 128), F32),
            pltpu.VMEM((ND, 128, 128), F32),
            pltpu.VMEM((128, 128), F32),
            pltpu.VMEM((NZ, 16, 128), F32),
            pltpu.VMEM((16, 128), F32),
            pltpu.VMEM((NY, 16, 128), F32),
            pltpu.VMEM((16, 128), F32),
            pltpu.VMEM((128, 128), F32),
            pltpu.VMEM((n, 128), F32),
            pltpu.SemaphoreType.DMA((5, 8)),
            pltpu.SemaphoreType.DMA((5, 8)),
        ],
        compiler_params=pltpu.CompilerParams(collective_id=2, has_side_effects=True),
        cost_estimate=cost(33),
        name="total",
    )(far, near)


def unpack_kernel(first_ref, lo_ref, hi_ref, b0, b1, b2, b3, out_ref):
    row = lax.broadcasted_iota(I32, (16, 128), 0)
    y, _ = place()
    for i, back_ref in enumerate((b0, b1, b2, b3)):

        def block(b, c, i=i, back_ref=back_ref):
            d = ((y - i) & (NY - 1)) * NZ + b
            first, lo, hi = first_ref[d], lo_ref[d], hi_ref[d]

            def tile(t, c):
                src = pl.ds(pl.multiple_of(t * 16, 16), 16)
                dst = pl.ds(pl.multiple_of(first + t * 16, 16), 16)
                at = row + t * 16
                new, old = back_ref[b, src, :].astype(F32), out_ref[dst, :].astype(F32)
                out_ref[dst, :] = jnp.where((at >= lo) & (at < hi), new, old).astype(BF16)
                return c

            def plain(t, c):
                src = pl.ds(pl.multiple_of(t * 16, 16), 16)
                out_ref[pl.ds(pl.multiple_of(first + t * 16, 16), 16), :] = back_ref[b, src, :]
                return c

            begin, end = (lo + 15) // 16, hi // 16
            fours = jnp.maximum(end - begin, 0) // 4

            def four(g, c):
                t = begin + g * 4
                src = pl.ds(pl.multiple_of(t * 16, 16), 64)
                out_ref[pl.ds(pl.multiple_of(first + t * 16, 16), 64), :] = back_ref[b, src, :]
                return c

            lax.fori_loop(0, fours, four, 0)
            lax.fori_loop(begin + fours * 4, end, plain, 0)
            lax.fori_loop(lo // 16, jnp.minimum(lo // 16 + 1, (hi + 15) // 16), tile, 0)
            lax.fori_loop(jnp.maximum(end, lo // 16 + 1), (hi + 15) // 16, tile, 0)
            return c

        lax.fori_loop(0, NZ, block, 0)


def unpack(first, lo, hi, back, rows):
    return pl.pallas_call(
        unpack_kernel,
        out_shape=jax.ShapeDtypeStruct((rows, 128), BF16),
        in_specs=[SM] * 3 + [VM] * NY,
        out_specs=VM,
        compiler_params=pltpu.CompilerParams(vmem_limit_bytes=VLIM),
        cost_estimate=cost(8),
        name="unpack",
    )(first, lo, hi, *back)


def per_device(features, child_parent, child_code, weight, out_grad):
    feats, cotangent = features[0], out_grad[0]
    fine_rows = feats.shape[0]
    as2d = lambda v: v.reshape(fine_rows // 128, 128)
    blocks, slots, rows, first, lo, hi = pack(as2d(child_parent[0]), as2d(child_code[0]), feats)
    table, want, got, near_blocks, parts = exchange(cotangent, rows, slots, blocks)

    def along_z(v, s):
        if s == 0:
            return v
        return lax.ppermute(v, "space", [(d, d // NZ * NZ + (d + s) % NZ) for d in range(NS)])

    def along_y(v, i):
        if i == 0:
            return v
        return lax.ppermute(v, "space", [(d, (d + i * NZ) % NS) for d in range(NS)])

    arrived = [along_z(v, s) for s, v in enumerate(parts)]
    table = table.reshape(NZ * PAR, 128)
    far, far_term = proxy((2, 1), want, table, weight, blocks, parts)
    near, near_term = proxy((3, 0), want, table, weight, blocks, parts)
    reply = {**far, **near}
    back = [along_y(reply[i], i) for i in range(NY)]
    grad_rows = fine_rows * NS * lax.axis_size("dp")
    weight_grad = total(far_term, near_term, float(1.0 / grad_rows**0.5))
    first, weight_grad = lax.optimization_barrier((first, weight_grad))
    feature_grad = unpack(first, lo, hi, back, fine_rows)
    got, feature_grad = lax.optimization_barrier((got, feature_grad))
    result = owner(got, weight.reshape(KINDS * 128, 128), blocks, near_blocks, arrived)
    return result[None], feature_grad[None], weight_grad.reshape(KINDS, 128, 128)


def solution(mesh):
    placed = (P("dp", "space", None), P("dp", "space"), P("dp", "space"), P(), P("dp", "space", None))
    return jax.shard_map(
        per_device,
        mesh=mesh,
        in_specs=placed,
        out_specs=(P("dp", "space", None), P("dp", "space", None), P()),
        check_vma=False,
    )
```

```python
import jax
import jax.numpy as jnp
from jax import lax
from jax.experimental import pallas as pl
from jax.experimental.pallas import tpu as pltpu
from jax.sharding import PartitionSpec as P


MESH = pl.DeviceIdType.MESH
NY = 4
NZ = 8
NS = NY * NZ
ND = 8
CAP = 528
KINDS = 8
PAR = 2048
SLOTS = KINDS * PAR
F32 = jnp.float32
BF16 = jnp.bfloat16
I32 = jnp.int32
ANY = pl.BlockSpec(memory_space=pl.ANY)
VM = pl.BlockSpec(memory_space=pltpu.VMEM)
SM = pl.BlockSpec(memory_space=pltpu.SMEM)
VLIM = 60 * 1024 * 1024
LATE = (3, 4, 5)


def cost(us):
    return pl.CostEstimate(flops=0, bytes_accessed=int(us * 3.6e6), transcendentals=0)


def pack_kernel(parent_ref, code_ref, feat_ref, blk_ref, slots_ref, rows_ref, first_ref, lo_ref, hi_ref, par, kind):
    step = pl.program_id(0)
    n = feat_ref.shape[0]

    @pl.when(step == 0)
    def _():
        whole = parent_ref[...]
        par[0 : n // 128, :] = whole
        kind[0 : n // 128, :] = code_ref[...]
        begin = jnp.int32(0)
        for d in range(NS):
            below = jnp.sum((whole < (d + 1) * PAR).astype(F32), axis=0, keepdims=True)
            end = jnp.sum(below).astype(I32)
            first = jnp.minimum(begin // 16 * 16, n - CAP)
            first_ref[d] = first
            lo_ref[d] = begin - first
            hi_ref[d] = end - first
            begin = end

    lane = lax.broadcasted_iota(I32, (8, 128), 1)
    pos = lax.broadcasted_iota(I32, (8, 128), 0) * 128 + lane

    def block(b, c):
        d = step * NZ + b
        first = pl.multiple_of(first_ref[d], 16)
        lo, hi = lo_ref[d], hi_ref[d]
        blk_ref[b] = feat_ref[pl.ds(first, CAP), :]
        at, lane0 = first // 128, lax.rem(first, 128)
        turn = lax.rem(128 - lane0, 128)
        live = (pos >= lo) & (pos < hi)

        def moved(ref):
            here = pltpu.roll(ref[pl.ds(at, 8), :], turn, 1)
            after = pltpu.roll(ref[pl.ds(at + 1, 8), :], turn, 1)
            return jnp.where(lane < 128 - lane0, here, after)

        parents, kinds = moved(par), moved(kind)

        def marked(v, other):
            v = jnp.where(live, v, other)
            return jnp.where(pos == 1022, lo, jnp.where(pos == 1023, hi, v))

        slots_ref[b] = marked(kinds * PAR + (parents & (PAR - 1)), SLOTS)
        rows_ref[b] = marked((parents & (NZ * PAR - 1)) + kinds * (NZ * PAR), SLOTS * NZ)
        return c

    lax.fori_loop(0, NZ, block, 0)


def pack(parents, codes, feats):
    rows = feats.shape[0]
    whole = lambda a: pl.BlockSpec(a.shape, lambda i: (0, 0))
    return pl.pallas_call(
        pack_kernel,
        out_shape=(
            jax.ShapeDtypeStruct((NS, CAP, 128), BF16),
            jax.ShapeDtypeStruct((NS, 8, 128), I32),
            jax.ShapeDtypeStruct((NS, 8, 128), I32),
        )
        + (jax.ShapeDtypeStruct((NS,), I32),) * 3,
        grid=(NY,),
        in_specs=[whole(parents), whole(codes), whole(feats)],
        out_specs=(
            pl.BlockSpec((NZ, CAP, 128), lambda i: (i, 0, 0)),
            pl.BlockSpec((NZ, 8, 128), lambda i: (i, 0, 0)),
            pl.BlockSpec((NZ, 8, 128), lambda i: (i, 0, 0)),
            SM,
            SM,
            SM,
        ),
        scratch_shapes=[pltpu.VMEM((rows // 128 + 16, 128), I32), pltpu.VMEM((rows // 128 + 16, 128), I32)],
        compiler_params=pltpu.CompilerParams(vmem_limit_bytes=VLIM),
        cost_estimate=cost(8),
        name="pack",
    )(parents, codes, feats)


def exchange_kernel(grad_ref, rows_ref, slots_ref, blk_ref, table_ref, want_ref, got_ref, near_ref, *rest):
    parts, (ss, rs, ys, yr, gs, gr, fs, fr, ns, nr, local) = rest[:NZ], rest[NZ:]
    dp, me = lax.axis_index("dp"), lax.axis_index("space")
    y, z = me // NZ, lax.rem(me, NZ)
    barrier = pltpu.get_barrier_semaphore()

    def greet(i, c):
        pl.semaphore_signal(barrier, inc=1, device_id=(dp, lax.rem(me + i, NS)), device_id_type=MESH)
        return c

    lax.fori_loop(1, NS, greet, 0)
    own = [
        pltpu.make_async_copy(grad_ref, table_ref.at[z], local.at[0]),
        pltpu.make_async_copy(rows_ref.at[pl.ds(y * NZ, NZ)], want_ref.at[pl.ds(y * NZ, NZ)], local.at[1]),
        pltpu.make_async_copy(slots_ref.at[me], got_ref.at[me], local.at[2]),
    ]
    for copy in own:
        copy.start()
    pl.semaphore_wait(barrier, NS - 1)
    half = PAR // 2

    def hop(k, side, sub):
        block = lax.rem(z - k + NZ, NZ) if side == 0 else lax.rem(z + k, NZ)
        to = lax.rem(z + 1, NZ) if side == 0 else lax.rem(z + NZ - 1, NZ)
        part = pl.ds(sub * half, half)
        src = grad_ref.at[part] if k == 0 else table_ref.at[block, part]
        return pltpu.make_async_remote_copy(
            src,
            table_ref.at[block, part],
            ss.at[side, k, sub],
            rs.at[side, k, sub],
            device_id=(dp, y * NZ + to),
            device_id_type=MESH,
        )

    chain = [(k, i) for k in range(4) for i in range(2 if k < 3 else 1)]
    hops = {(k, side, i): hop(k, side, side ^ i) for k, i in chain for side in range(2)}

    def rows_to(i):
        ty = lax.rem(y + i, NY)
        return pltpu.make_async_remote_copy(
            rows_ref.at[pl.ds(ty * NZ, NZ)],
            want_ref.at[pl.ds(y * NZ, NZ)],
            ys.at[i],
            yr.at[i],
            device_id=(dp, ty * NZ + z),
            device_id_type=MESH,
        )

    def block_to(i, r):
        ty = lax.rem(y + i, NY)
        return pltpu.make_async_remote_copy(
            blk_ref.at[ty * NZ + lax.rem(z + r, NZ)],
            parts[r].at[i - 1],
            fs.at[i, r],
            fr.at[i, r],
            device_id=(dp, ty * NZ + z),
            device_id_type=MESH,
        )

    moves = [block_to(i, r) for r in range(NZ) for i in range(1, NY)]

    def straight(r):
        tz = lax.rem(z + r, NZ)
        return pltpu.make_async_remote_copy(
            blk_ref.at[y * NZ + tz],
            near_ref.at[r],
            ns.at[r],
            nr.at[r],
            device_id=(dp, y * NZ + tz),
            device_id_type=MESH,
        )

    straights = [straight(r) for r in range(1, NZ) if r not in LATE]

    def slots_to(i):
        t = lax.rem(me + i, NS)
        return pltpu.make_async_remote_copy(
            slots_ref.at[t], got_ref.at[me], gs.at[i], gr.at[i], device_id=(dp, t), device_id_type=MESH
        )

    for i in range(2):
        for side in range(2):
            hops[0, side, i].start()
    for i in range(1, NY):
        rows_to(i).start()

    def start_slots(i, c):
        slots_to(i).start()
        return c

    lax.fori_loop(1, NS, start_slots, 0)
    for move in moves:
        move.start()
    for k, i in chain:
        if (k, i) == (2, 1):
            for move in straights:
                move.start()
        for side in range(2):
            hops[k, side, i].wait_recv()
            if (k + 1, side, i) in hops:
                hops[k + 1, side, i].start()
    for copy in hops.values():
        copy.wait_send()
    for move in moves + straights:
        move.wait()
    for i in range(1, NY):
        rows_to(i).wait()

    def end_slots(i, c):
        slots_to(i).wait()
        return c

    lax.fori_loop(1, NS, end_slots, 0)
    for copy in own:
        copy.wait()


def exchange(grad, rows, slots, blocks):
    ints = jax.ShapeDtypeStruct((NS, 8, 128), I32)
    part = jax.ShapeDtypeStruct((NY - 1, CAP, 128), BF16)
    near = jax.ShapeDtypeStruct((NZ, CAP, 128), BF16)
    dma = pltpu.SemaphoreType.DMA
    sems = [(2, 4, 2), (2, 4, 2), (NY,), (NY,), (NS,), (NS,), (NY, NZ), (NY, NZ), (NZ,), (NZ,), (3,)]
    out = pl.pallas_call(
        exchange_kernel,
        out_shape=(jax.ShapeDtypeStruct((NZ, PAR, 128), BF16), ints, ints, near) + (part,) * NZ,
        in_specs=[ANY] * 4,
        out_specs=(ANY,) * (4 + NZ),
        scratch_shapes=[dma(n) for n in sems],
        compiler_params=pltpu.CompilerParams(collective_id=1, has_side_effects=True),
        cost_estimate=cost(50),
        name="exchange",
    )(grad, rows, slots, blocks)
    return *out[:4], out[4:]


def place():
    me = lax.axis_index("space")
    return me >> 3, me & (NZ - 1)


def proxy_kernel(distances, want_ref, codes_ref, table_ref, weight_ref, blk_ref, *rest):
    n = len(distances)
    parts, outs = rest[:NZ], rest[NZ : NZ + n]
    term_ref, wide, rowbuf, feats, acc, turned_weight, sems = rest[NZ + n :]
    y, z = place()
    copies = [
        pltpu.make_async_copy(
            part.at[NY - 1 - i] if i else blk_ref.at[y * NZ + ((z + r) & (NZ - 1))], feats.at[r, m], sems.at[r, m]
        )
        for m, i in enumerate(distances)
        for r, part in enumerate(parts)
    ]
    for copy in copies:
        copy.start()
    acc[...] = jnp.zeros(acc.shape, F32)
    for k in range(KINDS):
        half, kk = k // 4, k % 4
        turned_weight[kk * 128 : (kk + 1) * 128, half * 128 : (half + 1) * 128] = jnp.transpose(weight_ref[k])

    def widen(i, c):
        at = pl.ds(pl.multiple_of(i * 512, 512), 512)
        wide[at, :] = table_ref[at, :].astype(F32)
        return c

    lax.fori_loop(0, NZ * PAR // 512, widen, 0)
    for copy in copies:
        copy.wait()

    for m, out_ref in enumerate(outs):
        q = (y + distances[m]) & (NY - 1)

        def block(r, c, m_at=m, q=q, out_ref=out_ref):
            zz = (z + r) & (NZ - 1)
            at = q * NZ + zz
            base = at * 1024
            lo, hi = want_ref[base + 1022], want_ref[base + 1023]

            def group(g, c):
                for u in range(16):
                    j = g * 16 + u
                    rowbuf[pl.ds(j, 1), :] = wide[pl.ds(want_ref[base + j] & (NZ * PAR - 1), 1), :]
                return c

            lax.fori_loop(lo // 16, (hi + 15) // 16, group, 0)
            codes = (codes_ref[at] >> 14).astype(F32)
            columns = jnp.transpose(codes)

            def piece(first, last):
                n = last - first
                cols = range(first // 128, (last + 127) // 128)
                tall = [min(128, last - m * 128) for m in cols]
                kinds = [jnp.broadcast_to(columns[:t, m : m + 1], (t, 128)) for m, t in zip(cols, tall)]
                kinds = jnp.concatenate(kinds, axis=0)
                upper = kinds >= 4.0
                quarter = jnp.where(upper, kinds - 4.0, kinds)
                rows = rowbuf[first:last, :]
                none = jnp.zeros(rows.shape, F32)
                placed = [jnp.where(quarter == kk, rows, none).astype(BF16) for kk in range(4)]
                placed = jnp.concatenate(placed, axis=1)
                both = jnp.dot(placed, turned_weight[...], preferred_element_type=F32)
                out_ref[zz, first:last, :] = jnp.where(upper, both[:, 128:], both[:, :128]).astype(BF16)
                turned = jnp.transpose(feats[r, m_at, first:last, :]).astype(F32)
                across = jnp.concatenate([codes[m : m + 1, :] for m in cols], axis=1)[:, :n]
                upper = jnp.broadcast_to(across, (128, n)) >= 4.0
                none = jnp.zeros((128, n), F32)
                split = [jnp.where(upper, none, turned).astype(BF16), jnp.where(upper, turned, none).astype(BF16)]
                acc[...] += jnp.dot(jnp.concatenate(split, axis=0), placed, preferred_element_type=F32)

            piece(0, 256)

            @pl.when(hi > 256)
            def _():
                piece(256, CAP)

            return c

        lax.fori_loop(0, NZ, block, 0)
    for k in range(KINDS):
        half, kk = k // 4, k % 4
        term_ref[k * 128 : (k + 1) * 128, :] = acc[half * 128 : (half + 1) * 128, kk * 128 : (kk + 1) * 128]


def proxy(distances, want, table, weight, blocks, parts):
    n = len(distances)
    *rows, term = pl.pallas_call(
        lambda *refs: proxy_kernel(distances, *refs),
        out_shape=(jax.ShapeDtypeStruct((NZ, CAP, 128), BF16),) * n
        + (jax.ShapeDtypeStruct((KINDS * 128, 128), F32),),
        in_specs=[SM, VM, VM, VM] + [ANY] * (NZ + 1),
        out_specs=(VM,) * (n + 1),
        scratch_shapes=[
            pltpu.VMEM((NZ * PAR, 128), F32),
            pltpu.VMEM((CAP, 128), F32),
            pltpu.VMEM((NZ, n, CAP, 128), BF16),
            pltpu.VMEM((256, 512), F32),
            pltpu.VMEM((512, 256), BF16),
            pltpu.SemaphoreType.DMA((NZ, n)),
        ],
        compiler_params=pltpu.CompilerParams(vmem_limit_bytes=VLIM),
        cost_estimate=cost(20),
        name="proxy",
    )(want.reshape(-1), want, table, weight, blocks, *parts)
    return dict(zip(distances, rows)), term


def owner_kernel(slot_ref, weight_ref, blk_ref, near_ref, late_ref, *rest):
    parts = rest[:NZ]
    out_ref, grid_ref, rowbuf, feats, sems = rest[NZ:]
    y, z = place()

    def straight(s):
        if s == 0:
            return blk_ref.at[y * NZ + z]
        return late_ref.at[LATE.index(s)] if s in LATE else near_ref.at[s]

    copies = [
        (
            pltpu.make_async_copy(part, feats.at[s, pl.ds(1, NY - 1)], sems.at[s, 0]),
            pltpu.make_async_copy(straight(s), feats.at[s, 0], sems.at[s, 1]),
        )
        for s, part in enumerate(parts)
    ]
    for pair in copies:
        for copy in pair:
            copy.start()

    def clear(i, c):
        grid_ref[pl.ds(pl.multiple_of(i * 512, 512), 512), :] = jnp.zeros((512, 128), F32)
        return c

    lax.fori_loop(0, SLOTS // 512, clear, 0)

    for s in range(NZ):
        for copy in copies[s]:
            copy.wait()

        def block(i, c, s=s):
            base = (((y - i) & (NY - 1)) * NZ + ((z - s) & (NZ - 1))) * 1024
            lo, hi = slot_ref[base + 1022], slot_ref[base + 1023]
            rowbuf[...] = feats[s, i].astype(F32)

            def group(g, c):
                for u in range(16):
                    j = g * 16 + u
                    grid_ref[pl.ds(slot_ref[base + j], 1), :] = rowbuf[pl.ds(j, 1), :]
                return c

            lax.fori_loop(lo // 16, (hi + 15) // 16, group, 0)
            return c

        lax.fori_loop(0, NY, block, 0)

    def chunk(i, c):
        total = jnp.zeros((512, 128), F32)
        for k in range(0, KINDS, 2):
            pair = [grid_ref[pl.ds(pl.multiple_of(m * PAR + i * 512, 512), 512), :].astype(BF16) for m in (k, k + 1)]
            kids = jnp.concatenate(pair, axis=1)
            total = total + jnp.dot(kids, weight_ref[k * 128 : (k + 2) * 128, :], preferred_element_type=F32)
        out_ref[pl.ds(pl.multiple_of(i * 512, 512), 512), :] = total.astype(BF16)
        return c

    lax.fori_loop(0, PAR // 512, chunk, 0)


def owner(slots, weight, blocks, near, late, parts):
    return pl.pallas_call(
        owner_kernel,
        out_shape=jax.ShapeDtypeStruct((PAR, 128), BF16),
        in_specs=[SM, VM] + [ANY] * (NZ + 3),
        out_specs=VM,
        scratch_shapes=[
            pltpu.VMEM((SLOTS + 8, 128), F32),
            pltpu.VMEM((CAP, 128), F32),
            pltpu.VMEM((NZ, NY, CAP, 128), BF16),
            pltpu.SemaphoreType.DMA((NZ, 2)),
        ],
        compiler_params=pltpu.CompilerParams(vmem_limit_bytes=VLIM),
        cost_estimate=cost(18),
        name="owner",
    )(slots.reshape(-1), weight, blocks, near, late, *parts)


def total_kernel(
    scale, far_ref, near_ref, blk_ref, out_ref, late_ref, term_ref, b1, s1, b2, s2, b3, s3, b4, s4, send, recv, ls, lr
):
    dp, me = lax.axis_index("dp"), lax.axis_index("space")
    y, z = me // NZ, lax.rem(me, NZ)
    at_dp = lambda i: (lax.rem(dp + i, ND), me)
    at_z = lambda i: (dp, y * NZ + lax.rem(z + i, NZ))
    at_y = lambda i: (dp, lax.rem(y + i, NY) * NZ + z)
    term_ref[...] = far_ref[...] + near_ref[...]
    barrier = pltpu.get_barrier_semaphore()
    for who, n in ((at_dp, ND), (at_z, NZ), (at_y, NY)):
        for i in range(1, n):
            pl.semaphore_signal(barrier, inc=1, device_id=who(i), device_id_type=MESH)
    pl.semaphore_wait(barrier, ND + NZ + NY - 3)

    def swap(phase, n, who, src, dst):
        copies = [
            pltpu.make_async_remote_copy(
                src(i), dst, send.at[phase, i], recv.at[phase, i], device_id=who(i), device_id_type=MESH
            )
            for i in range(1, n)
        ]
        for c in copies:
            c.start()
        return copies

    def end(copies):
        for c in copies:
            c.wait()

    def rows(i, n):
        return pl.ds(pl.multiple_of(i * n, n), n)

    c = swap(0, ND, at_dp, lambda i: term_ref.at[rows(lax.rem(dp + i, ND), 128)], b1.at[dp])
    b1[dp] = term_ref[rows(dp, 128), :]
    end(c)
    s1[...] = ((b1[0] + b1[1]) + (b1[2] + b1[3])) + ((b1[4] + b1[5]) + (b1[6] + b1[7]))
    c = swap(1, NZ, at_z, lambda i: s1.at[rows(lax.rem(z + i, NZ), 16)], b2.at[z])
    b2[z] = s1[rows(z, 16), :]
    end(c)
    s2[...] = ((b2[0] + b2[1]) + (b2[2] + b2[3])) + ((b2[4] + b2[5]) + (b2[6] + b2[7]))
    c = swap(2, NY, at_y, lambda i: s2, b3.at[y])
    b3[y] = s2[...]
    end(c)
    s3[...] = ((b3[0] + b3[1]) + (b3[2] + b3[3])) * scale
    c = swap(3, NZ, at_z, lambda i: s3, b4.at[rows(z, 16)])
    late = [
        pltpu.make_async_remote_copy(
            blk_ref.at[y * NZ + lax.rem(z + r, NZ)],
            late_ref.at[m],
            ls.at[m],
            lr.at[m],
            device_id=at_z(r),
            device_id_type=MESH,
        )
        for m, r in enumerate(LATE)
    ]
    for copy in late:
        copy.start()
    b4[rows(z, 16), :] = s3[...]
    end(c)
    c = swap(4, ND, at_dp, lambda i: b4, s4.at[rows(dp, 128)])
    s4[rows(dp, 128), :] = b4[...]
    end(c)
    out_ref[...] = s4[...]
    end(late)


def total(far, near, blocks, scale):
    n = KINDS * 128
    return pl.pallas_call(
        lambda *refs: total_kernel(scale, *refs),
        out_shape=(
            jax.ShapeDtypeStruct((n, 128), F32),
            jax.ShapeDtypeStruct((len(LATE), CAP, 128), BF16),
        ),
        in_specs=[VM, VM, ANY],
        out_specs=(VM, ANY),
        scratch_shapes=[
            pltpu.VMEM((n, 128), F32),
            pltpu.VMEM((ND, 128, 128), F32),
            pltpu.VMEM((128, 128), F32),
            pltpu.VMEM((NZ, 16, 128), F32),
            pltpu.VMEM((16, 128), F32),
            pltpu.VMEM((NY, 16, 128), F32),
            pltpu.VMEM((16, 128), F32),
            pltpu.VMEM((128, 128), F32),
            pltpu.VMEM((n, 128), F32),
            pltpu.SemaphoreType.DMA((5, 8)),
            pltpu.SemaphoreType.DMA((5, 8)),
            pltpu.SemaphoreType.DMA((len(LATE),)),
            pltpu.SemaphoreType.DMA((len(LATE),)),
        ],
        compiler_params=pltpu.CompilerParams(collective_id=2, has_side_effects=True),
        cost_estimate=cost(33),
        name="total",
    )(far, near, blocks)


def unpack_kernel(first_ref, lo_ref, hi_ref, b0, b1, b2, b3, out_ref):
    row = lax.broadcasted_iota(I32, (16, 128), 0)
    y, _ = place()
    for i, back_ref in enumerate((b0, b1, b2, b3)):

        def block(b, c, i=i, back_ref=back_ref):
            d = ((y - i) & (NY - 1)) * NZ + b
            first, lo, hi = first_ref[d], lo_ref[d], hi_ref[d]

            def tile(t, c):
                src = pl.ds(pl.multiple_of(t * 16, 16), 16)
                dst = pl.ds(pl.multiple_of(first + t * 16, 16), 16)
                at = row + t * 16
                new, old = back_ref[b, src, :].astype(F32), out_ref[dst, :].astype(F32)
                out_ref[dst, :] = jnp.where((at >= lo) & (at < hi), new, old).astype(BF16)
                return c

            def plain(t, c):
                src = pl.ds(pl.multiple_of(t * 16, 16), 16)
                out_ref[pl.ds(pl.multiple_of(first + t * 16, 16), 16), :] = back_ref[b, src, :]
                return c

            begin, end = (lo + 15) // 16, hi // 16
            fours = jnp.maximum(end - begin, 0) // 4

            def four(g, c):
                t = begin + g * 4
                src = pl.ds(pl.multiple_of(t * 16, 16), 64)
                out_ref[pl.ds(pl.multiple_of(first + t * 16, 16), 64), :] = back_ref[b, src, :]
                return c

            lax.fori_loop(0, fours, four, 0)
            lax.fori_loop(begin + fours * 4, end, plain, 0)
            lax.fori_loop(lo // 16, jnp.minimum(lo // 16 + 1, (hi + 15) // 16), tile, 0)
            lax.fori_loop(jnp.maximum(end, lo // 16 + 1), (hi + 15) // 16, tile, 0)
            return c

        lax.fori_loop(0, NZ, block, 0)


def unpack(first, lo, hi, back, rows):
    return pl.pallas_call(
        unpack_kernel,
        out_shape=jax.ShapeDtypeStruct((rows, 128), BF16),
        in_specs=[SM] * 3 + [VM] * NY,
        out_specs=VM,
        compiler_params=pltpu.CompilerParams(vmem_limit_bytes=VLIM),
        cost_estimate=cost(8),
        name="unpack",
    )(first, lo, hi, *back)


def per_device(features, child_parent, child_code, weight, out_grad):
    feats, cotangent = features[0], out_grad[0]
    fine_rows = feats.shape[0]
    as2d = lambda v: v.reshape(fine_rows // 128, 128)
    blocks, slots, rows, first, lo, hi = pack(as2d(child_parent[0]), as2d(child_code[0]), feats)
    table, want, got, near_blocks, parts = exchange(cotangent, rows, slots, blocks)

    def along_z(v, s):
        if s == 0:
            return v
        return lax.ppermute(v, "space", [(d, d // NZ * NZ + (d + s) % NZ) for d in range(NS)])

    def along_y(v, i):
        if i == 0:
            return v
        return lax.ppermute(v, "space", [(d, (d + i * NZ) % NS) for d in range(NS)])

    arrived = [along_z(v, s) for s, v in enumerate(parts)]
    table = table.reshape(NZ * PAR, 128)
    far, far_term = proxy((2, 1), want, table, weight, blocks, parts)
    near, near_term = proxy((3, 0), want, table, weight, blocks, parts)
    reply = {**far, **near}
    back = [along_y(reply[i], i) for i in range(NY)]
    grad_rows = fine_rows * NS * lax.axis_size("dp")
    weight_grad, late_blocks = total(far_term, near_term, blocks, float(1.0 / grad_rows**0.5))
    first, weight_grad = lax.optimization_barrier((first, weight_grad))
    feature_grad = unpack(first, lo, hi, back, fine_rows)
    got, feature_grad = lax.optimization_barrier((got, feature_grad))
    result = owner(got, weight.reshape(KINDS * 128, 128), blocks, near_blocks, late_blocks, arrived)
    return result[None], feature_grad[None], weight_grad.reshape(KINDS, 128, 128)


def solution(mesh):
    placed = (P("dp", "space", None), P("dp", "space"), P("dp", "space"), P(), P("dp", "space", None))
    return jax.shard_map(
        per_device,
        mesh=mesh,
        in_specs=placed,
        out_specs=(P("dp", "space", None), P("dp", "space", None), P()),
        check_vma=False,
    )
```

```python
import jax
import jax.numpy as jnp
from jax import lax
from jax.experimental import pallas as pl
from jax.experimental.pallas import tpu as pltpu
from jax.sharding import PartitionSpec as P


MESH = pl.DeviceIdType.MESH
NY = 4
NZ = 8
NS = NY * NZ
ND = 8
CAP = 528
KINDS = 8
PAR = 2048
SLOTS = KINDS * PAR
F32 = jnp.float32
BF16 = jnp.bfloat16
I32 = jnp.int32
ANY = pl.BlockSpec(memory_space=pl.ANY)
VM = pl.BlockSpec(memory_space=pltpu.VMEM)
SM = pl.BlockSpec(memory_space=pltpu.SMEM)
VLIM = 60 * 1024 * 1024
LATE = (3, 4, 5)


def cost(us):
    return pl.CostEstimate(flops=0, bytes_accessed=int(us * 3.6e6), transcendentals=0)


def pack_kernel(parent_ref, code_ref, feat_ref, blk_ref, slots_ref, rows_ref, first_ref, lo_ref, hi_ref, par, kind):
    step = pl.program_id(0)
    n = feat_ref.shape[0]

    @pl.when(step == 0)
    def _():
        whole = parent_ref[...]
        par[0 : n // 128, :] = whole
        kind[0 : n // 128, :] = code_ref[...]
        begin = jnp.int32(0)
        for d in range(NS):
            below = jnp.sum((whole < (d + 1) * PAR).astype(F32), axis=0, keepdims=True)
            end = jnp.sum(below).astype(I32)
            first = jnp.minimum(begin // 16 * 16, n - CAP)
            first_ref[d] = first
            lo_ref[d] = begin - first
            hi_ref[d] = end - first
            begin = end

    lane = lax.broadcasted_iota(I32, (8, 128), 1)
    pos = lax.broadcasted_iota(I32, (8, 128), 0) * 128 + lane

    def block(b, c):
        d = step * NZ + b
        first = pl.multiple_of(first_ref[d], 16)
        lo, hi = lo_ref[d], hi_ref[d]
        blk_ref[b] = feat_ref[pl.ds(first, CAP), :]
        at, lane0 = first // 128, lax.rem(first, 128)
        turn = lax.rem(128 - lane0, 128)
        live = (pos >= lo) & (pos < hi)

        def moved(ref):
            here = pltpu.roll(ref[pl.ds(at, 8), :], turn, 1)
            after = pltpu.roll(ref[pl.ds(at + 1, 8), :], turn, 1)
            return jnp.where(lane < 128 - lane0, here, after)

        parents, kinds = moved(par), moved(kind)

        def marked(v, other):
            v = jnp.where(live, v, other)
            return jnp.where(pos == 1022, lo, jnp.where(pos == 1023, hi, v))

        slots_ref[b] = marked(kinds * PAR + (parents & (PAR - 1)), SLOTS)
        rows_ref[b] = marked((parents & (NZ * PAR - 1)) + kinds * (NZ * PAR), SLOTS * NZ)
        return c

    lax.fori_loop(0, NZ, block, 0)


def pack(parents, codes, feats):
    rows = feats.shape[0]
    whole = lambda a: pl.BlockSpec(a.shape, lambda i: (0, 0))
    return pl.pallas_call(
        pack_kernel,
        out_shape=(
            jax.ShapeDtypeStruct((NS, CAP, 128), BF16),
            jax.ShapeDtypeStruct((NS, 8, 128), I32),
            jax.ShapeDtypeStruct((NS, 8, 128), I32),
        )
        + (jax.ShapeDtypeStruct((NS,), I32),) * 3,
        grid=(NY,),
        in_specs=[whole(parents), whole(codes), whole(feats)],
        out_specs=(
            pl.BlockSpec((NZ, CAP, 128), lambda i: (i, 0, 0)),
            pl.BlockSpec((NZ, 8, 128), lambda i: (i, 0, 0)),
            pl.BlockSpec((NZ, 8, 128), lambda i: (i, 0, 0)),
            SM,
            SM,
            SM,
        ),
        scratch_shapes=[pltpu.VMEM((rows // 128 + 16, 128), I32), pltpu.VMEM((rows // 128 + 16, 128), I32)],
        compiler_params=pltpu.CompilerParams(vmem_limit_bytes=VLIM),
        cost_estimate=cost(8),
        name="pack",
    )(parents, codes, feats)


def exchange_kernel(grad_ref, rows_ref, slots_ref, blk_ref, table_ref, want_ref, got_ref, near_ref, *rest):
    parts, (ss, rs, ys, yr, gs, gr, fs, fr, ns, nr, local) = rest[:NZ], rest[NZ:]
    dp, me = lax.axis_index("dp"), lax.axis_index("space")
    y, z = me // NZ, lax.rem(me, NZ)
    barrier = pltpu.get_barrier_semaphore()

    def greet(i, c):
        pl.semaphore_signal(barrier, inc=1, device_id=(dp, lax.rem(me + i, NS)), device_id_type=MESH)
        return c

    lax.fori_loop(1, NS, greet, 0)
    own = [
        pltpu.make_async_copy(grad_ref, table_ref.at[z], local.at[0]),
        pltpu.make_async_copy(rows_ref.at[pl.ds(y * NZ, NZ)], want_ref.at[pl.ds(y * NZ, NZ)], local.at[1]),
        pltpu.make_async_copy(slots_ref.at[me], got_ref.at[me], local.at[2]),
    ]
    for copy in own:
        copy.start()
    pl.semaphore_wait(barrier, NS - 1)
    half = PAR // 2

    def hop(k, side, sub):
        block = lax.rem(z - k + NZ, NZ) if side == 0 else lax.rem(z + k, NZ)
        to = lax.rem(z + 1, NZ) if side == 0 else lax.rem(z + NZ - 1, NZ)
        part = pl.ds(sub * half, half)
        src = grad_ref.at[part] if k == 0 else table_ref.at[block, part]
        return pltpu.make_async_remote_copy(
            src,
            table_ref.at[block, part],
            ss.at[side, k, sub],
            rs.at[side, k, sub],
            device_id=(dp, y * NZ + to),
            device_id_type=MESH,
        )

    chain = [(k, i) for k in range(4) for i in range(2 if k < 3 else 1)]
    hops = {(k, side, i): hop(k, side, side ^ i) for k, i in chain for side in range(2)}

    def rows_to(i):
        ty = lax.rem(y + i, NY)
        return pltpu.make_async_remote_copy(
            rows_ref.at[pl.ds(ty * NZ, NZ)],
            want_ref.at[pl.ds(y * NZ, NZ)],
            ys.at[i],
            yr.at[i],
            device_id=(dp, ty * NZ + z),
            device_id_type=MESH,
        )

    def block_to(i, r):
        ty = lax.rem(y + i, NY)
        return pltpu.make_async_remote_copy(
            blk_ref.at[ty * NZ + lax.rem(z + r, NZ)],
            parts[r].at[i - 1],
            fs.at[i, r],
            fr.at[i, r],
            device_id=(dp, ty * NZ + z),
            device_id_type=MESH,
        )

    moves = [block_to(i, r) for r in range(NZ) for i in range(1, NY)]

    def straight(r):
        tz = lax.rem(z + r, NZ)
        return pltpu.make_async_remote_copy(
            blk_ref.at[y * NZ + tz],
            near_ref.at[r],
            ns.at[r],
            nr.at[r],
            device_id=(dp, y * NZ + tz),
            device_id_type=MESH,
        )

    straights = [straight(r) for r in range(1, NZ) if r not in LATE]

    def slots_to(i):
        t = lax.rem(me + i, NS)
        return pltpu.make_async_remote_copy(
            slots_ref.at[t], got_ref.at[me], gs.at[i], gr.at[i], device_id=(dp, t), device_id_type=MESH
        )

    for i in range(2):
        for side in range(2):
            hops[0, side, i].start()
    for i in range(1, NY):
        rows_to(i).start()

    def start_slots(i, c):
        slots_to(i).start()
        return c

    lax.fori_loop(1, NS, start_slots, 0)
    for move in moves:
        move.start()
    for k, i in chain:
        if (k, i) == (2, 1):
            for move in straights:
                move.start()
        for side in range(2):
            hops[k, side, i].wait_recv()
            if (k + 1, side, i) in hops:
                hops[k + 1, side, i].start()
    for copy in hops.values():
        copy.wait_send()
    for move in moves + straights:
        move.wait()
    for i in range(1, NY):
        rows_to(i).wait()

    def end_slots(i, c):
        slots_to(i).wait()
        return c

    lax.fori_loop(1, NS, end_slots, 0)
    for copy in own:
        copy.wait()


def exchange(grad, rows, slots, blocks):
    ints = jax.ShapeDtypeStruct((NS, 8, 128), I32)
    part = jax.ShapeDtypeStruct((NY - 1, CAP, 128), BF16)
    near = jax.ShapeDtypeStruct((NZ, CAP, 128), BF16)
    dma = pltpu.SemaphoreType.DMA
    sems = [(2, 4, 2), (2, 4, 2), (NY,), (NY,), (NS,), (NS,), (NY, NZ), (NY, NZ), (NZ,), (NZ,), (3,)]
    out = pl.pallas_call(
        exchange_kernel,
        out_shape=(jax.ShapeDtypeStruct((NZ, PAR, 128), BF16), ints, ints, near) + (part,) * NZ,
        in_specs=[ANY] * 4,
        out_specs=(ANY,) * (4 + NZ),
        scratch_shapes=[dma(n) for n in sems],
        compiler_params=pltpu.CompilerParams(collective_id=1, has_side_effects=True),
        cost_estimate=cost(50),
        name="exchange",
    )(grad, rows, slots, blocks)
    return *out[:4], out[4:]


def place():
    me = lax.axis_index("space")
    return me >> 3, me & (NZ - 1)


def proxy_kernel(distances, want_ref, codes_ref, table_ref, weight_ref, blk_ref, *rest):
    n = len(distances)
    parts, outs = rest[:NZ], rest[NZ : NZ + n]
    term_ref, wide, rowbuf, feats, acc, turned_weight, sems = rest[NZ + n :]
    y, z = place()
    copies = [
        pltpu.make_async_copy(
            part.at[NY - 1 - i] if i else blk_ref.at[y * NZ + ((z + r) & (NZ - 1))], feats.at[r, m], sems.at[r, m]
        )
        for m, i in enumerate(distances)
        for r, part in enumerate(parts)
    ]
    for copy in copies:
        copy.start()
    acc[...] = jnp.zeros(acc.shape, F32)
    for k in range(KINDS):
        half, kk = k // 4, k % 4
        turned_weight[kk * 128 : (kk + 1) * 128, half * 128 : (half + 1) * 128] = jnp.transpose(weight_ref[k])

    def widen(i, c):
        at = pl.ds(pl.multiple_of(i * 512, 512), 512)
        wide[at, :] = table_ref[at, :].astype(F32)
        return c

    lax.fori_loop(0, NZ * PAR // 512, widen, 0)
    for copy in copies:
        copy.wait()

    for m, out_ref in enumerate(outs):
        q = (y + distances[m]) & (NY - 1)

        def block(r, c, m_at=m, q=q, out_ref=out_ref):
            zz = (z + r) & (NZ - 1)
            at = q * NZ + zz
            base = at * 1024
            lo, hi = want_ref[base + 1022], want_ref[base + 1023]

            def group(g, c):
                for u in range(16):
                    j = g * 16 + u
                    rowbuf[pl.ds(j, 1), :] = wide[pl.ds(want_ref[base + j] & (NZ * PAR - 1), 1), :]
                return c

            lax.fori_loop(lo // 16, (hi + 15) // 16, group, 0)
            codes = (codes_ref[at] >> 14).astype(F32)
            columns = jnp.transpose(codes)

            def piece(first, last):
                n = last - first
                cols = range(first // 128, (last + 127) // 128)
                tall = [min(128, last - m * 128) for m in cols]
                kinds = [jnp.broadcast_to(columns[:t, m : m + 1], (t, 128)) for m, t in zip(cols, tall)]
                kinds = jnp.concatenate(kinds, axis=0)
                upper = kinds >= 4.0
                quarter = jnp.where(upper, kinds - 4.0, kinds)
                rows = rowbuf[first:last, :]
                none = jnp.zeros(rows.shape, F32)
                placed = [jnp.where(quarter == kk, rows, none).astype(BF16) for kk in range(4)]
                placed = jnp.concatenate(placed, axis=1)
                both = jnp.dot(placed, turned_weight[...], preferred_element_type=F32)
                out_ref[zz, first:last, :] = jnp.where(upper, both[:, 128:], both[:, :128]).astype(BF16)
                turned = jnp.transpose(feats[r, m_at, first:last, :]).astype(F32)
                across = jnp.concatenate([codes[m : m + 1, :] for m in cols], axis=1)[:, :n]
                upper = jnp.broadcast_to(across, (128, n)) >= 4.0
                none = jnp.zeros((128, n), F32)
                split = [jnp.where(upper, none, turned).astype(BF16), jnp.where(upper, turned, none).astype(BF16)]
                acc[...] += jnp.dot(jnp.concatenate(split, axis=0), placed, preferred_element_type=F32)

            piece(0, 256)

            @pl.when(hi > 256)
            def _():
                piece(256, CAP)

            return c

        lax.fori_loop(0, NZ, block, 0)
    for k in range(KINDS):
        half, kk = k // 4, k % 4
        term_ref[k * 128 : (k + 1) * 128, :] = acc[half * 128 : (half + 1) * 128, kk * 128 : (kk + 1) * 128]


def proxy(distances, want, table, weight, blocks, parts):
    n = len(distances)
    *rows, term = pl.pallas_call(
        lambda *refs: proxy_kernel(distances, *refs),
        out_shape=(jax.ShapeDtypeStruct((NZ, CAP, 128), BF16),) * n
        + (jax.ShapeDtypeStruct((KINDS * 128, 128), F32),),
        in_specs=[SM, VM, VM, VM] + [ANY] * (NZ + 1),
        out_specs=(VM,) * (n + 1),
        scratch_shapes=[
            pltpu.VMEM((NZ * PAR, 128), F32),
            pltpu.VMEM((CAP, 128), F32),
            pltpu.VMEM((NZ, n, CAP, 128), BF16),
            pltpu.VMEM((256, 512), F32),
            pltpu.VMEM((512, 256), BF16),
            pltpu.SemaphoreType.DMA((NZ, n)),
        ],
        compiler_params=pltpu.CompilerParams(vmem_limit_bytes=VLIM),
        cost_estimate=cost(20),
        name="proxy",
    )(want.reshape(-1), want, table, weight, blocks, *parts)
    return dict(zip(distances, rows)), term


def owner_kernel(slot_ref, weight_ref, blk_ref, near_ref, late_ref, *rest):
    parts = rest[:NZ]
    out_ref, grid_ref, rowbuf, feats, sems = rest[NZ:]
    y, z = place()

    def straight(s):
        if s == 0:
            return blk_ref.at[y * NZ + z]
        return late_ref.at[LATE.index(s)] if s in LATE else near_ref.at[s]

    copies = [
        (
            pltpu.make_async_copy(part, feats.at[s, pl.ds(1, NY - 1)], sems.at[s, 0]),
            pltpu.make_async_copy(straight(s), feats.at[s, 0], sems.at[s, 1]),
        )
        for s, part in enumerate(parts)
    ]
    for pair in copies:
        for copy in pair:
            copy.start()

    def clear(i, c):
        grid_ref[pl.ds(pl.multiple_of(i * 512, 512), 512), :] = jnp.zeros((512, 128), F32)
        return c

    lax.fori_loop(0, SLOTS // 512, clear, 0)

    for s in range(NZ):
        for copy in copies[s]:
            copy.wait()

        def block(i, c, s=s):
            base = (((y - i) & (NY - 1)) * NZ + ((z - s) & (NZ - 1))) * 1024
            lo, hi = slot_ref[base + 1022], slot_ref[base + 1023]
            rowbuf[...] = feats[s, i].astype(F32)

            def group(g, c):
                for u in range(16):
                    j = g * 16 + u
                    grid_ref[pl.ds(slot_ref[base + j], 1), :] = rowbuf[pl.ds(j, 1), :]
                return c

            lax.fori_loop(lo // 16, (hi + 15) // 16, group, 0)
            return c

        lax.fori_loop(0, NY, block, 0)

    def chunk(i, c):
        total = jnp.zeros((512, 128), F32)
        for k in range(0, KINDS, 2):
            pair = [grid_ref[pl.ds(pl.multiple_of(m * PAR + i * 512, 512), 512), :].astype(BF16) for m in (k, k + 1)]
            kids = jnp.concatenate(pair, axis=1)
            total = total + jnp.dot(kids, weight_ref[k * 128 : (k + 2) * 128, :], preferred_element_type=F32)
        out_ref[pl.ds(pl.multiple_of(i * 512, 512), 512), :] = total.astype(BF16)
        return c

    lax.fori_loop(0, PAR // 512, chunk, 0)


def owner(slots, weight, blocks, near, late, parts):
    return pl.pallas_call(
        owner_kernel,
        out_shape=jax.ShapeDtypeStruct((PAR, 128), BF16),
        in_specs=[SM, VM] + [ANY] * (NZ + 3),
        out_specs=VM,
        scratch_shapes=[
            pltpu.VMEM((SLOTS + 8, 128), F32),
            pltpu.VMEM((CAP, 128), F32),
            pltpu.VMEM((NZ, NY, CAP, 128), BF16),
            pltpu.SemaphoreType.DMA((NZ, 2)),
        ],
        compiler_params=pltpu.CompilerParams(vmem_limit_bytes=VLIM),
        cost_estimate=cost(18),
        name="owner",
    )(slots.reshape(-1), weight, blocks, near, late, *parts)


def total_kernel(
    scale, far_ref, near_ref, blk_ref, out_ref, late_ref, term_ref, b1, s1, b2, s2, b3, s3, b4, s4, send, recv, ls, lr
):
    dp, me = lax.axis_index("dp"), lax.axis_index("space")
    y, z = me // NZ, lax.rem(me, NZ)
    at_dp = lambda i: (lax.rem(dp + i, ND), me)
    at_z = lambda i: (dp, y * NZ + lax.rem(z + i, NZ))
    at_y = lambda i: (dp, lax.rem(y + i, NY) * NZ + z)
    term_ref[...] = far_ref[...] + near_ref[...]
    barrier = pltpu.get_barrier_semaphore()
    for who, n in ((at_dp, ND), (at_z, NZ), (at_y, NY)):
        for i in range(1, n):
            pl.semaphore_signal(barrier, inc=1, device_id=who(i), device_id_type=MESH)
    pl.semaphore_wait(barrier, ND + NZ + NY - 3)

    def swap(phase, n, who, src, dst):
        copies = [
            pltpu.make_async_remote_copy(
                src(i), dst, send.at[phase, i], recv.at[phase, i], device_id=who(i), device_id_type=MESH
            )
            for i in range(1, n)
        ]
        for c in copies:
            c.start()
        return copies

    def end(copies):
        for c in copies:
            c.wait()

    def rows(i, n):
        return pl.ds(pl.multiple_of(i * n, n), n)

    c = swap(0, ND, at_dp, lambda i: term_ref.at[rows(lax.rem(dp + i, ND), 128)], b1.at[dp])
    b1[dp] = term_ref[rows(dp, 128), :]
    end(c)
    s1[...] = ((b1[0] + b1[1]) + (b1[2] + b1[3])) + ((b1[4] + b1[5]) + (b1[6] + b1[7]))
    c = swap(1, NZ, at_z, lambda i: s1.at[rows(lax.rem(z + i, NZ), 16)], b2.at[z])
    late = [
        pltpu.make_async_remote_copy(
            blk_ref.at[y * NZ + lax.rem(z + r, NZ)],
            late_ref.at[m],
            ls.at[m],
            lr.at[m],
            device_id=at_z(r),
            device_id_type=MESH,
        )
        for m, r in enumerate(LATE)
    ]
    late[1].start()
    b2[z] = s1[rows(z, 16), :]
    end(c)
    s2[...] = ((b2[0] + b2[1]) + (b2[2] + b2[3])) + ((b2[4] + b2[5]) + (b2[6] + b2[7]))
    c = swap(2, NY, at_y, lambda i: s2, b3.at[y])
    b3[y] = s2[...]
    end(c)
    s3[...] = ((b3[0] + b3[1]) + (b3[2] + b3[3])) * scale
    c = swap(3, NZ, at_z, lambda i: s3, b4.at[rows(z, 16)])
    for m in (0, 2):
        late[m].start()
    b4[rows(z, 16), :] = s3[...]
    end(c)
    c = swap(4, ND, at_dp, lambda i: b4, s4.at[rows(dp, 128)])
    s4[rows(dp, 128), :] = b4[...]
    end(c)
    out_ref[...] = s4[...]
    end(late)


def total(far, near, blocks, scale):
    n = KINDS * 128
    return pl.pallas_call(
        lambda *refs: total_kernel(scale, *refs),
        out_shape=(
            jax.ShapeDtypeStruct((n, 128), F32),
            jax.ShapeDtypeStruct((len(LATE), CAP, 128), BF16),
        ),
        in_specs=[VM, VM, ANY],
        out_specs=(VM, ANY),
        scratch_shapes=[
            pltpu.VMEM((n, 128), F32),
            pltpu.VMEM((ND, 128, 128), F32),
            pltpu.VMEM((128, 128), F32),
            pltpu.VMEM((NZ, 16, 128), F32),
            pltpu.VMEM((16, 128), F32),
            pltpu.VMEM((NY, 16, 128), F32),
            pltpu.VMEM((16, 128), F32),
            pltpu.VMEM((128, 128), F32),
            pltpu.VMEM((n, 128), F32),
            pltpu.SemaphoreType.DMA((5, 8)),
            pltpu.SemaphoreType.DMA((5, 8)),
            pltpu.SemaphoreType.DMA((len(LATE),)),
            pltpu.SemaphoreType.DMA((len(LATE),)),
        ],
        compiler_params=pltpu.CompilerParams(collective_id=2, has_side_effects=True),
        cost_estimate=cost(33),
        name="total",
    )(far, near, blocks)


def unpack_kernel(first_ref, lo_ref, hi_ref, b0, b1, b2, b3, out_ref):
    row = lax.broadcasted_iota(I32, (16, 128), 0)
    y, _ = place()
    for i, back_ref in enumerate((b0, b1, b2, b3)):

        def block(b, c, i=i, back_ref=back_ref):
            d = ((y - i) & (NY - 1)) * NZ + b
            first, lo, hi = first_ref[d], lo_ref[d], hi_ref[d]

            def tile(t, c):
                src = pl.ds(pl.multiple_of(t * 16, 16), 16)
                dst = pl.ds(pl.multiple_of(first + t * 16, 16), 16)
                at = row + t * 16
                new, old = back_ref[b, src, :].astype(F32), out_ref[dst, :].astype(F32)
                out_ref[dst, :] = jnp.where((at >= lo) & (at < hi), new, old).astype(BF16)
                return c

            def plain(t, c):
                src = pl.ds(pl.multiple_of(t * 16, 16), 16)
                out_ref[pl.ds(pl.multiple_of(first + t * 16, 16), 16), :] = back_ref[b, src, :]
                return c

            begin, end = (lo + 15) // 16, hi // 16
            fours = jnp.maximum(end - begin, 0) // 4

            def four(g, c):
                t = begin + g * 4
                src = pl.ds(pl.multiple_of(t * 16, 16), 64)
                out_ref[pl.ds(pl.multiple_of(first + t * 16, 16), 64), :] = back_ref[b, src, :]
                return c

            lax.fori_loop(0, fours, four, 0)
            lax.fori_loop(begin + fours * 4, end, plain, 0)
            lax.fori_loop(lo // 16, jnp.minimum(lo // 16 + 1, (hi + 15) // 16), tile, 0)
            lax.fori_loop(jnp.maximum(end, lo // 16 + 1), (hi + 15) // 16, tile, 0)
            return c

        lax.fori_loop(0, NZ, block, 0)


def unpack(first, lo, hi, back, rows):
    return pl.pallas_call(
        unpack_kernel,
        out_shape=jax.ShapeDtypeStruct((rows, 128), BF16),
        in_specs=[SM] * 3 + [VM] * NY,
        out_specs=VM,
        compiler_params=pltpu.CompilerParams(vmem_limit_bytes=VLIM),
        cost_estimate=cost(8),
        name="unpack",
    )(first, lo, hi, *back)


def per_device(features, child_parent, child_code, weight, out_grad):
    feats, cotangent = features[0], out_grad[0]
    fine_rows = feats.shape[0]
    as2d = lambda v: v.reshape(fine_rows // 128, 128)
    blocks, slots, rows, first, lo, hi = pack(as2d(child_parent[0]), as2d(child_code[0]), feats)
    table, want, got, near_blocks, parts = exchange(cotangent, rows, slots, blocks)

    def along_z(v, s):
        if s == 0:
            return v
        return lax.ppermute(v, "space", [(d, d // NZ * NZ + (d + s) % NZ) for d in range(NS)])

    def along_y(v, i):
        if i == 0:
            return v
        return lax.ppermute(v, "space", [(d, (d + i * NZ) % NS) for d in range(NS)])

    arrived = [along_z(v, s) for s, v in enumerate(parts)]
    table = table.reshape(NZ * PAR, 128)
    far, far_term = proxy((2, 1), want, table, weight, blocks, parts)
    near, near_term = proxy((3, 0), want, table, weight, blocks, parts)
    reply = {**far, **near}
    back = [along_y(reply[i], i) for i in range(NY)]
    grad_rows = fine_rows * NS * lax.axis_size("dp")
    weight_grad, late_blocks = total(far_term, near_term, blocks, float(1.0 / grad_rows**0.5))
    first, weight_grad = lax.optimization_barrier((first, weight_grad))
    feature_grad = unpack(first, lo, hi, back, fine_rows)
    got, feature_grad = lax.optimization_barrier((got, feature_grad))
    result = owner(got, weight.reshape(KINDS * 128, 128), blocks, near_blocks, late_blocks, arrived)
    return result[None], feature_grad[None], weight_grad.reshape(KINDS, 128, 128)


def solution(mesh):
    placed = (P("dp", "space", None), P("dp", "space"), P("dp", "space"), P(), P("dp", "space", None))
    return jax.shard_map(
        per_device,
        mesh=mesh,
        in_specs=placed,
        out_specs=(P("dp", "space", None), P("dp", "space", None), P()),
        check_vma=False,
    )
```
